32 devices in a mesh: dp: 4 (over z), fsdp: 8 (over y, x, core).
Axes of the slice: x: 2, y: 2, z: 4, core: 2. Of those that a mesh axis runs over, the one named last changes fastest.
Arguments:
- inputs: bfloat16 [2, 20480, 768], P(None, ('dp', 'fsdp')), may hold values from -6 to 6
- cotangent: bfloat16 [2, 20480, 768], P(None, ('dp', 'fsdp')), may hold values from -6 to 6
- qkv_weight: bfloat16 [768, 2304], P(('dp', 'fsdp')), may hold values from -0.21875 to 0.21875
- proj_weight: bfloat16 [768, 768], P(('dp', 'fsdp')), may hold values from -1.5 to 1.5
- expand_weight: bfloat16 [768, 2304], P(('dp', 'fsdp')), may hold values from -0.21875 to 0.21875
- contract_weight: bfloat16 [1152, 768], P(None, ('dp', 'fsdp')), may hold values from -0.1875 to 0.1875
- prenorm: bfloat16 [768], P(('dp', 'fsdp')), may hold values from 0.5 to 1.5
- midnorm: bfloat16 [768], P(('dp', 'fsdp')), may hold values from 0.5 to 1.5
- lengths: int32 [2, 4, 8], P(None, 'dp'), may hold values from 1 to 20, as said below
- dealing: int32 [2, 160], P(None, ('dp', 'fsdp')), may hold values from 0 to 159, as said below
- holders: int32 [2, 2, 160], P(None, None, ('dp', 'fsdp')), may hold values from 0 to 5, as said below
- counts: int32 [2, 160], P(None, ('dp', 'fsdp')), may hold values from 1 to 128, as said below
Outputs:
- result: bfloat16 [2, 20480, 768], P(None, ('dp', 'fsdp'))
- input_grad: bfloat16 [2, 20480, 768], P(None, ('dp', 'fsdp'))
- grad_qkv: float32 [768, 2304], P(('dp', 'fsdp'))
- grad_proj: float32 [768, 768], P(('dp', 'fsdp'))
- grad_expand: float32 [768, 2304], P(('dp', 'fsdp'))
- grad_contract: float32 [1152, 768], P(None, ('dp', 'fsdp'))
- grad_prenorm: float32 [768], P(('dp', 'fsdp'))
- grad_midnorm: float32 [768], P(('dp', 'fsdp'))
The draws below stay inside these ranges and needn't reach their ends.
Inputs may be any that keep to these rules, and one draw needn't show every extreme that they name: lengths[m, g] are the block counts of 8 sequences laid end to end over the 40 blocks of dp index g; they sum to 40 and one of them is 20. `dealing`: the 5 slots of device d hold a permutation of its own blocks, numbered in sequence order d * 5 to d * 5 + 4. holders[m, 0, s] is the slot number on the same device of block dealing[m, s] - 1, or 5 where dealing[m, s] is the device's first block in sequence order; holders[m, 1, s] is the slot number on the same device of block dealing[m, s] + 1, or 5 where dealing[m, s] is the device's last block in sequence order. counts[m, o] is 128 except for the last block of a sequence.
All inputs are finite; a program needn't handle non-finite values.
Results may differ from the reference program's by a relative error of at most 0.015.
Values may be sent and summed in bfloat16 or wider, within the bound.
A program may use at most 256 MiB of HBM per device.

```python
from functools import partial
import jax
import jax.numpy as jnp
from jax import lax

D = 768
HEADS = 12
HEAD_DIM = 64
FF = 1152
BLK = 128
BLK_MB = 5
MB = 2
NSEQ = 8
TOKENS = 20480
GROUP_BLOCKS = 40
LONGEST = 20
N_DP = 4
N_FSDP = 8
DEVICES = 32


def split_lengths(key):
    group_blocks = BLK_MB * N_FSDP
    remainder = group_blocks - LONGEST
    others = NSEQ - 1
    base_share = remainder // others
    leftover = remainder % others

    def one_group(group_key):
        shares = base_share + (jnp.arange(others) < leftover).astype(jnp.int32)
        step_keys = jax.random.split(group_key, others + 1)
        for pair_idx in range(others // 2):
            first_share = shares[2 * pair_idx]
            second_share = shares[2 * pair_idx + 1]
            lowest = jnp.maximum(first_share - LONGEST, 1 - second_share)
            highest = jnp.minimum(first_share - 1, LONGEST - second_share)
            transfer = jax.random.randint(step_keys[pair_idx], (), lowest, highest + 1)
            shares = shares.at[2 * pair_idx].add(-transfer).at[2 * pair_idx + 1].add(transfer)
        complete = jnp.concatenate([jnp.full((1,), LONGEST, jnp.int32), shares.astype(jnp.int32)])
        return complete[jax.random.permutation(step_keys[others], NSEQ)]
    group_keys = jax.random.split(jax.random.fold_in(key, 7), MB * N_DP)
    return jax.vmap(one_group)(group_keys).reshape(MB, N_DP, NSEQ).astype(jnp.int32)


def draw_lengths(key, part):
    return split_lengths(key)


def draw_counts(key, part):
    seq_blocks = split_lengths(key)
    group_blocks = BLK_MB * N_FSDP
    seq_ends = jnp.cumsum(seq_blocks, axis=-1) - 1
    block_ids = jnp.arange(group_blocks)
    is_last = jnp.any(block_ids[None, None, :, None] == seq_ends[:, :, None, :], axis=-1)
    partial_rows = jax.random.randint(jax.random.fold_in(key, 9), (MB, N_DP, group_blocks), 1, BLK + 1)
    return jnp.where(is_last, partial_rows, BLK).reshape(MB, BLK_MB * DEVICES).astype(jnp.int32)


def deal_blocks(key):
    device_keys = jax.random.split(jax.random.fold_in(key, 5), MB * DEVICES)
    within = jax.vmap(lambda device_key: jax.random.permutation(device_key, BLK_MB))(device_keys)
    return within.reshape(MB, DEVICES, BLK_MB).astype(jnp.int32)


def draw_dealing(key, part):
    within = deal_blocks(key)
    base_ids = (jnp.arange(DEVICES, dtype=jnp.int32) * BLK_MB)[None, :, None]
    return (within + base_ids).reshape(MB, DEVICES * BLK_MB).astype(jnp.int32)


def draw_holders(key, part):
    within = deal_blocks(key)
    inverse = jnp.argsort(within, axis=-1).astype(jnp.int32)
    previous = jnp.take_along_axis(inverse, jnp.maximum(within - 1, 0), axis=-1)
    following = jnp.take_along_axis(inverse, jnp.minimum(within + 1, BLK_MB - 1), axis=-1)
    prev_slot = jnp.where(within == 0, BLK_MB, previous).reshape(MB, DEVICES * BLK_MB)
    next_slot = jnp.where(within == BLK_MB - 1, BLK_MB, following).reshape(MB, DEVICES * BLK_MB)
    return jnp.stack([prev_slot, next_slot], axis=1).astype(jnp.int32)


def raised(values, own_key, source, target, shards_of, factor):
    owner, partner = [(jnp.arange(values.shape[position]) // (values.shape[position] // shards_of)).reshape([-1 if axis == position else 1 for axis in range(values.ndim)]) for position in (source, target)]
    chosen = jax.random.permutation(own_key, shards_of)[partner]
    strong = (owner == chosen) | (owner == (partner + shards_of // 2) % shards_of)
    return jnp.where(strong, factor * values, values)


def shard_levels(own_key, extent, pieces, low, top_value):
    level, own = 1.0, jax.random.fold_in(own_key, 6)
    for axis_at, parts in pieces:
        heights = jnp.exp(jax.random.uniform(jax.random.fold_in(own, axis_at), (parts,), jnp.float32, low / len(pieces), top_value / len(pieces)))
        level = level * jnp.repeat(heights, extent[axis_at] // parts).reshape([-1 if axis == axis_at else 1 for axis in range(len(extent))])
    return level


def bell_draw(own_key, extent, scale, bound, cuts=(), kind=jnp.bfloat16):
    factor_of = shard_levels(own_key, extent, cuts, -0.22, 0.18) if cuts else 1.0
    entries = jax.random.normal(own_key, extent, jnp.float32) * scale * factor_of
    return jnp.minimum(jnp.maximum(entries, -bound), bound).astype(kind)


def noise_with(rng, shape, deviation, limit, pieces, heavy, held_as=jnp.bfloat16):
    array = deviation * jax.random.normal(rng, shape, jnp.float32)
    if pieces:
        array = array * shard_levels(rng, shape, pieces, -0.22, 0.18)
    return jnp.clip(raised(array, jax.random.fold_in(rng, 3), *heavy), -limit, limit).astype(held_as)


def setup_inputs(seed: int = 0) -> dict:
    arg_keys = jax.random.split(jax.random.key(seed), 13)
    inputs = bell_draw(arg_keys[0], (MB, TOKENS, D), 1.0, 6.0, ((1, 32),))
    cotangent = noise_with(arg_keys[1], (MB, TOKENS, D), 1.0, 6.0, ((1, 32),), (1, 2, 32, 2.75))
    qkv_weight = bell_draw(arg_keys[2], (D, 3 * D), D ** -0.5, 0.21875, ((0, 32),))
    proj_weight = bell_draw(arg_keys[3], (D, D), (D // 48) ** -0.5, 1.5, ((0, 32),))
    expand_weight = bell_draw(arg_keys[4], (D, 2 * FF), D ** -0.5, 0.21875, ((0, 32),))
    contract_weight = bell_draw(arg_keys[5], (FF, D), FF ** -0.5, 0.1875, ((1, 32),))
    prenorm = jnp.clip(1.0 + 0.1 * jax.random.normal(arg_keys[6], (D,), jnp.float32), 0.5, 1.5).astype(jnp.bfloat16)
    midnorm = jnp.clip(1.0 + 0.1 * jax.random.normal(arg_keys[7], (D,), jnp.float32), 0.5, 1.5).astype(jnp.bfloat16)
    lengths = draw_lengths(jax.random.fold_in(arg_keys[12], 71), 0)
    dealing = draw_dealing(jax.random.fold_in(arg_keys[12], 71), 0)
    holders = draw_holders(jax.random.fold_in(arg_keys[12], 71), 0)
    counts = draw_counts(jax.random.fold_in(arg_keys[12], 71), 0)
    return {"inputs": inputs, "cotangent": cotangent, "qkv_weight": qkv_weight, "proj_weight": proj_weight, "expand_weight": expand_weight, "contract_weight": contract_weight, "prenorm": prenorm, "midnorm": midnorm, "lengths": lengths, "dealing": dealing, "holders": holders, "counts": counts}


norm_epsilon = 1e-05
rope_base = 10000.0
masked_score = -1e+30

@jax.custom_vjp
def low(v):
    return lax.optimization_barrier(v.astype(jnp.bfloat16)).astype(jnp.float32)

@jax.custom_vjp
def low_back(v):
    return v

def low_keep(v):
    return (low(v), None)

def low_pass(kept, grad):
    return (grad,)

def back_keep(v):
    return (v, None)

def back_low(kept, grad):
    return (low(grad),)
low.defvjp(low_keep, low_pass)
low_back.defvjp(back_keep, back_low)

def layer_norm(values, gains):
    centred = values - lax.optimization_barrier(jnp.mean(values, axis=-1, keepdims=True))
    spread = lax.optimization_barrier(jnp.mean(centred * centred, axis=-1, keepdims=True))
    return centred * lax.rsqrt(spread + norm_epsilon) * gains

def rotate_half(values):
    halfway = values.shape[-1] // 2
    return jnp.concatenate([-values[..., halfway:], values[..., :halfway]], axis=-1)

def rope_tables(positions, head_size):
    halfway = head_size // 2
    exponents = jnp.arange(halfway, dtype=jnp.float32) * (2.0 / head_size)
    frequency = rope_base ** (-exponents)
    angles = positions[:, None] * frequency[None, :]
    angles = jnp.concatenate([angles, angles], axis=-1)
    return (jnp.cos(angles)[:, None, :], jnp.sin(angles)[:, None, :])

def apply_rope(values, cos_table, sin_table):
    return values * cos_table + rotate_half(values) * sin_table

def geglu(expanded):
    halfway = expanded.shape[-1] // 2
    return jax.nn.gelu(expanded[:, :halfway], approximate=False) * expanded[:, halfway:]

def window_mask(has_prev, has_next, key_valid, block_rows):
    half_rows = block_rows // 2
    query_row = jnp.arange(block_rows)[:, None]
    key_col = jnp.arange(2 * block_rows)[None, :]
    relative = key_col - query_row
    inside = (relative >= 0) & (relative <= block_rows)
    before_ok = (key_col >= half_rows)[None] | has_prev[:, None, None]
    after_ok = (key_col < half_rows + block_rows)[None] | has_next[:, None, None]
    return (inside[None] & before_ok & after_ok & (key_valid[:, None, :] > 0))[:, None]

def slot_layout(dealt_blocks, seq_starts, seq_lasts, group_blocks, valid_rows, block_rows):
    within = dealt_blocks % group_blocks
    begin = lax.optimization_barrier(jnp.max(jnp.where(seq_starts <= within[:, None], seq_starts, 0), axis=1))
    offset = within - begin
    is_last = jnp.any(seq_lasts == within[:, None], axis=1)
    row_ids = jnp.arange(block_rows)
    positions = (offset[:, None] * block_rows + row_ids[None, :]).reshape(-1).astype(jnp.float32)
    row_mask = (row_ids[None, :] < valid_rows[:, None]).astype(jnp.float32).reshape(-1, 1)
    return (offset > 0, jnp.logical_not(is_last), positions, row_mask)

def attend_packed(packed):
    query_tiles, key_tiles, value_tiles, allowed = packed
    highest = lax.Precision.HIGHEST
    score_scale = HEAD_DIM ** (-0.5)
    scores = jnp.einsum('brhe,bche->bhrc', query_tiles, key_tiles, precision=highest) * score_scale
    scores = low_back(jnp.where(allowed, scores, masked_score))
    attn_probs = low(jax.nn.softmax(scores, axis=-1))
    return jnp.einsum('bhrc,bche->brhe', attn_probs, value_tiles, precision=highest)

def layer_forward(row_mask, cos_table, sin_table, pred_index, succ_index, allowed, x_rows, w_qkv, w_proj, w_expand, w_contract, gain_pre, gain_mid):
    highest = lax.Precision.HIGHEST
    row_count = x_rows.shape[0]
    block_count = pred_index.shape[0]
    device_count = block_count // BLK_MB
    half_rows = BLK // 2
    normed_one = low(layer_norm(x_rows, gain_pre))
    qkv_full = low_back(jnp.dot(normed_one, w_qkv, precision=highest)).reshape(row_count, 3, HEADS, HEAD_DIM)
    query_rot = low(apply_rope(qkv_full[:, 0], cos_table, sin_table))
    key_rot = low(apply_rope(qkv_full[:, 1], cos_table, sin_table))
    value_own = low(qkv_full[:, 2])
    key_blocks = key_rot.reshape(block_count, BLK, HEADS, HEAD_DIM)
    value_blocks = value_own.reshape(block_count, BLK, HEADS, HEAD_DIM)
    key_tiles = jnp.concatenate([key_blocks[pred_index][:, half_rows:], key_blocks, key_blocks[succ_index][:, :half_rows]], axis=1)
    value_tiles = jnp.concatenate([value_blocks[pred_index][:, half_rows:], value_blocks, value_blocks[succ_index][:, :half_rows]], axis=1)
    query_tiles = query_rot.reshape(block_count, BLK, HEADS, HEAD_DIM)
    packed = tuple((tensor.reshape((device_count, BLK_MB) + tensor.shape[1:]) for tensor in (query_tiles, key_tiles, value_tiles, allowed)))
    attended = lax.map(jax.checkpoint(attend_packed), packed)
    attended = low(low_back(attended.reshape(row_count, HEADS * HEAD_DIM)))
    attn_branch = low_back(jnp.dot(attended, w_proj, precision=highest))
    mid_rows = x_rows + row_mask * attn_branch
    normed_two = low(layer_norm(mid_rows, gain_mid))
    expanded = low_back(jnp.dot(normed_two, w_expand, precision=highest))
    hidden = low(geglu(expanded))
    ffn_branch = low_back(jnp.dot(hidden, w_contract, precision=highest))
    return mid_rows + row_mask * ffn_branch

def group_step(params, grad_sums, packed):
    inputs_group, cotangent_group, dealt_blocks, holder_row, count_row, seq_blocks = packed
    group_blocks = dealt_blocks.shape[0]
    half_rows = BLK // 2
    local_orig = dealt_blocks % BLK_MB
    valid_rows = jnp.take(count_row, (dealt_blocks % group_blocks).astype(jnp.int32))
    seq_ends = jnp.cumsum(seq_blocks)
    seq_starts = jnp.broadcast_to((seq_ends - seq_blocks)[None, :], (group_blocks, seq_blocks.shape[0]))
    seq_lasts = jnp.broadcast_to((seq_ends - 1)[None, :], (group_blocks, seq_blocks.shape[0]))
    has_prev, has_next, positions, row_mask = slot_layout(dealt_blocks, seq_starts, seq_lasts, group_blocks, valid_rows, BLK)
    cos_table, sin_table = rope_tables(positions, HEAD_DIM)
    device_of = jnp.arange(group_blocks) // BLK_MB
    group_devices = group_blocks // BLK_MB
    last_of = lax.optimization_barrier(jnp.sum(jnp.where(local_orig.reshape(-1, BLK_MB) == BLK_MB - 1, jnp.arange(BLK_MB)[None, :], 0), axis=1))
    first_of = lax.optimization_barrier(jnp.sum(jnp.where(local_orig.reshape(-1, BLK_MB) == 0, jnp.arange(BLK_MB)[None, :], 0), axis=1))
    before = jnp.maximum(device_of - 1, 0)
    after = jnp.minimum(device_of + 1, group_devices - 1)
    pred_index = jnp.where(holder_row[0] < BLK_MB, device_of * BLK_MB + holder_row[0], before * BLK_MB + last_of[before]).astype(jnp.int32)
    succ_index = jnp.where(holder_row[1] < BLK_MB, device_of * BLK_MB + holder_row[1], after * BLK_MB + first_of[after]).astype(jnp.int32)
    mask_blocks = row_mask.reshape(group_blocks, BLK)
    key_valid = jnp.concatenate([jnp.ones((group_blocks, half_rows), jnp.float32), mask_blocks, mask_blocks[succ_index][:, :half_rows]], axis=1)
    allowed = window_mask(has_prev, has_next, key_valid, BLK)
    forward = partial(layer_forward, row_mask, cos_table, sin_table, pred_index, succ_index, allowed)
    outcome, pullback = jax.vjp(forward, inputs_group.astype(jnp.float32), *params)
    gradients = pullback(cotangent_group.astype(jnp.float32))
    new_sums = tuple((running + increment for running, increment in zip(grad_sums, gradients[1:])))
    return (new_sums, (outcome.astype(jnp.bfloat16), gradients[0].astype(jnp.bfloat16)))

def reference(inputs, cotangent, qkv_weight, proj_weight, expand_weight, contract_weight, prenorm, midnorm, lengths, dealing, holders, counts):
    params = tuple((tensor.astype(jnp.float32) for tensor in (qkv_weight, proj_weight, expand_weight, contract_weight, prenorm, midnorm)))
    grad_sums = tuple((jnp.zeros(tensor.shape, jnp.float32) for tensor in params))
    group_rows = GROUP_BLOCKS * BLK
    results = []
    input_grads = []
    for batch_idx in range(MB):
        holder_groups = jnp.transpose(holders[batch_idx].reshape(2, N_DP, GROUP_BLOCKS), (1, 0, 2))
        packed = (inputs[batch_idx].reshape(N_DP, group_rows, D), cotangent[batch_idx].reshape(N_DP, group_rows, D), dealing[batch_idx].reshape(N_DP, GROUP_BLOCKS), holder_groups, counts[batch_idx].reshape(N_DP, GROUP_BLOCKS), lengths[batch_idx])
        grad_sums, (result_groups, grad_groups) = lax.scan(partial(group_step, params), grad_sums, packed)
        results.append(result_groups.reshape(TOKENS, D))
        input_grads.append(grad_groups.reshape(TOKENS, D))
    return (jnp.stack(results), jnp.stack(input_grads), grad_sums[0], grad_sums[1], grad_sums[2], grad_sums[3], grad_sums[4], grad_sums[5])
```

```python
import functools

import jax
import jax.numpy as jnp
import numpy as np
from jax import lax
from jax.experimental import pallas as pl
from jax.experimental.pallas import tpu as pltpu
from jax.sharding import PartitionSpec as P

HEAD_DIM = 64
PAIR = 128
STEP_SLOTS = 2
CHUNK = 32
norm_epsilon = 1e-05
rope_base = 10000.0
masked_score = -1e30
F32 = jnp.float32
BF16 = jnp.bfloat16
VMEM_LIMIT = 60 * 1024 * 1024


def nn(a, b):
    return lax.dot_general(a, b, (((1,), (0,)), ((), ())), preferred_element_type=F32)


def nt(a, b):
    return lax.dot_general(a, b, (((1,), (1,)), ((), ())), preferred_element_type=F32)


def tn(a, b):
    return lax.dot_general(a, b, (((0,), (0,)), ((), ())), preferred_element_type=F32)


def rope_tables(most_offset, block_rows):
    half = HEAD_DIM // 2
    freq = rope_base ** (-np.arange(half) * (2.0 / HEAD_DIM))
    freq = np.tile(freq, PAIR // half)
    sign = np.where(np.arange(PAIR) % HEAD_DIM < half, -1.0, 1.0)

    def pair(positions):
        angles = positions[:, None] * freq[None, :]
        return (
            jnp.asarray(np.cos(angles), F32),
            jnp.asarray(np.sin(angles) * sign[None, :], F32),
        )

    return (*pair(np.arange(most_offset) * float(block_rows)), *pair(np.arange(block_rows) * 1.0))


def slot_scalars(lengths, dealing, slot, blocks, group):
    micro = slot // blocks
    place = slot - micro * blocks
    block = dealing[micro, place]
    within = lax.rem(block, group)
    begin = jnp.int32(0)
    start = jnp.int32(0)
    ends = jnp.int32(0)
    for seq in range(lengths.shape[1]):
        begin = jnp.where(start <= within, start, begin)
        start = start + lengths[micro, seq]
        ends = ends + jnp.where(start - 1 == within, 1, 0)
    return micro, place, lax.rem(block, blocks), within - begin, ends > 0


def slot_angles(offset, ca, sa, cb, sb):
    first_c, first_s = ca[pl.ds(offset, 1), :], sa[pl.ds(offset, 1), :]
    return first_c * cb[...] - first_s * sb[...], first_s * cb[...] + first_c * sb[...]


def swap_halves(v):
    low = lax.broadcasted_iota(jnp.int32, v.shape, 1) % HEAD_DIM < HEAD_DIM // 2
    return jnp.where(low, pltpu.roll(v, PAIR - HEAD_DIM // 2, 1), pltpu.roll(v, HEAD_DIM // 2, 1))


def head_masks(dtype):
    low = lax.broadcasted_iota(jnp.int32, (1, PAIR), 1) < HEAD_DIM
    return low.astype(F32).astype(dtype), (1.0 - low.astype(F32)).astype(dtype)


def two_heads(tile):
    even, odd = head_masks(tile.dtype)
    return jnp.concatenate([tile * even, tile * odd], axis=0)


def from_heads(t, rows):
    return jnp.concatenate([t[:HEAD_DIM, :rows], t[HEAD_DIM:, rows:]], axis=0).T


def chunk_rows(c, size=CHUNK):
    return pl.ds(pl.multiple_of(c * size, size), size)


def qkv_kernel(
    blocks, group, rows, width,
    lengths, dealing, counts, x, w_all, gain, ca, sa, cb, sb,
    q, k, v, normed, to_next, to_prev,
    w, full, cos, sin, sem,
):
    step = pl.program_id(0)
    half = rows // 2

    @pl.when(step == 0)
    def _():
        copy = pltpu.make_async_copy(w_all.at[:, pl.ds(0, 3 * width)], w, sem)
        copy.start()
        copy.wait()

    slots = [slot_scalars(lengths, dealing, step * STEP_SLOTS + t, blocks, group) for t in range(STEP_SLOTS)]
    for t, (_, _, _, offset, _) in enumerate(slots):
        c, s = slot_angles(offset, ca, sa, cb, sb)
        cos[t * rows : (t + 1) * rows, :] = c
        sin[t * rows : (t + 1) * rows, :] = s

    def norm(c, carry):
        at = chunk_rows(c)
        xf = x[at, :].astype(F32)
        centred = xf - jnp.mean(xf, axis=-1, keepdims=True)
        spread = jnp.mean(centred * centred, axis=-1, keepdims=True)
        normed[at, :] = (centred * lax.rsqrt(spread + norm_epsilon) * gain[...]).astype(BF16)
        return carry

    lax.fori_loop(0, STEP_SLOTS * rows // CHUNK, norm, 0)
    for n in range(0, 3 * width, 256):
        full[:, n : n + 256] = nn(normed[...], w[:, n : n + 256])

    def turn(c, carry):
        at = chunk_rows(c)
        co, si = cos[at, :], sin[at, :]
        for p in range(width // PAIR):
            lanes = slice(p * PAIR, (p + 1) * PAIR)
            for out, base in ((q, 0), (k, width)):
                tile = full[at, base + p * PAIR : base + (p + 1) * PAIR]
                out[at, lanes] = (tile * co + swap_halves(tile) * si).astype(BF16)
            v[at, lanes] = full[at, 2 * width + p * PAIR : 2 * width + (p + 1) * PAIR].astype(BF16)
        return carry

    lax.fori_loop(0, STEP_SLOTS * rows // CHUNK, turn, 0)
    for t, (micro, _, local, _, _) in enumerate(slots):
        base = t * rows

        @pl.when(local == blocks - 1)
        def _(micro=micro, base=base):
            to_next[micro, :half, :] = k[base + half : base + rows, :]
            to_next[micro, half:, :] = v[base + half : base + rows, :]

        @pl.when(local == 0)
        def _(micro=micro, base=base):
            to_prev[micro, :half, :] = k[base : base + half, :]
            to_prev[micro, half:rows, :] = v[base : base + half, :]
            valid = jnp.full((16, width), counts[micro, 0], jnp.int32).astype(F32)
            to_prev[micro, rows:, :] = valid.astype(BF16)


def layer_kernel(
    blocks, group, rows, width, hidden_units,
    lengths, dealing, holders, counts,
    q, k, v, from_prev, from_next, x, cot, w_all, gain, ca, sa, cb, sb,
    result, mid_grad, dq, hid, ffn_grad, normed, exp_grad, attended, attn_grad,
    dk, dv, back_prev, back_next, mid_term,
    wp, we, wc, kt, vt, bias, probs, expanded, wide, mid, hat, root, att_grad, tiles, sem,
):
    step = pl.program_id(0)
    half = rows // 2
    total = STEP_SLOTS * rows
    pairs = width // PAIR

    def weights():
        at = 3 * width
        out = []
        for place, (dst, cols) in enumerate(((we, 2 * hidden_units), (wc, hidden_units), (wp, width))):
            out.append(pltpu.make_async_copy(w_all.at[:, pl.ds(at, cols)], dst, sem.at[place]))
            at += cols
        return out

    @pl.when(step == 0)
    def _():
        for copy in weights():
            copy.start()
        dk[...] = jnp.zeros_like(dk)
        dv[...] = jnp.zeros_like(dv)
        mid_term[...] = jnp.zeros_like(mid_term)

    slots = []
    for t in range(STEP_SLOTS):
        slot = step * STEP_SLOTS + t
        micro, place, local, offset, is_last = slot_scalars(lengths, dealing, slot, blocks, group)
        pred, succ = holders[micro * 2, place], holders[micro * 2 + 1, place]
        count = counts[micro, local]
        slots.append((slot, micro, pred, succ, offset, count))
        for src, dst, part in ((k, kt, 0), (v, vt, half)):
            @pl.when(pred < blocks)
            def _(src=src, dst=dst, t=t, micro=micro, pred=pred):
                dst[t, :half, :] = src[micro * blocks + pred, half:, :]

            @pl.when(pred >= blocks)
            def _(dst=dst, part=part, t=t, micro=micro):
                dst[t, :half, :] = from_prev[micro, part : part + half, :]

            dst[t, half : half + rows, :] = src[slot]

            @pl.when(succ < blocks)
            def _(src=src, dst=dst, t=t, micro=micro, succ=succ):
                dst[t, half + rows :, :] = src[micro * blocks + succ, :half, :]

            @pl.when(succ >= blocks)
            def _(dst=dst, part=part, t=t, micro=micro):
                dst[t, half + rows :, :] = from_next[micro, part : part + half, :]

        col = lax.broadcasted_iota(jnp.int32, (2 * rows, rows), 0)
        row = lax.broadcasted_iota(jnp.int32, (2 * rows, rows), 1)
        follow = counts[micro, lax.rem(local + 1, blocks)]
        remote = from_next[micro, rows : rows + 1, :rows].astype(F32)
        follow = jnp.where(succ < blocks, jnp.full((1, rows), follow, jnp.int32).astype(F32), remote)
        follow = half + rows + jnp.minimum(follow, half)
        ends = jnp.full((1, rows), half + count, jnp.int32).astype(F32)
        high = jnp.where(is_last, ends, follow)
        lowest = jnp.where(offset > 0, 0, half)
        allowed = (col >= row) & (col - row <= rows) & (col >= lowest) & (col.astype(F32) < high)
        bias[t] = jnp.where(allowed, 0.0, masked_score)

    def attend(p, carry):
        lanes = pl.ds(pl.multiple_of(p * PAIR, PAIR), PAIR)
        for t in range(STEP_SLOTS):
            at = slice(t * rows, (t + 1) * rows)
            queries = two_heads(q[at, lanes] * jnp.asarray(HEAD_DIM**-0.5, BF16))
            scores = nt(kt[t, :, lanes], queries)
            scores = scores + jnp.concatenate([bias[t], bias[t]], axis=1)
            lifted = jnp.exp(scores - jnp.max(scores, axis=0, keepdims=True))
            prob = lifted * (1.0 / jnp.sum(lifted, axis=0, keepdims=True))
            probs[t, p] = prob
            mixed = tn(vt[t, :, lanes], prob.astype(BF16))
            attended[at, lanes] = from_heads(mixed, rows).astype(BF16)
        return carry

    lax.fori_loop(0, pairs, attend, 0)

    @pl.when(step == 0)
    def _():
        for copy in weights():
            copy.wait()

    def valid(c):
        per = rows // CHUNK
        inside = lax.rem(c, per) * CHUNK
        count = jnp.where(c < per, slots[0][5], slots[1][5])
        r = lax.broadcasted_iota(jnp.int32, (CHUNK, width), 0) + inside
        return r < count

    for n in range(0, width, 256):
        wide[:, n : n + 256] = nn(attended[...], wp[:, n : n + 256])

    def mid_norm(c, carry):
        at = chunk_rows(c)
        m = x[at, :].astype(F32) + jnp.where(valid(c), wide[at, :], 0.0)
        mid[at, :] = m
        centred = m - jnp.mean(m, axis=-1, keepdims=True)
        spread = jnp.mean(centred * centred, axis=-1, keepdims=True)
        scale = lax.rsqrt(spread + norm_epsilon)
        h = centred * scale
        hat[at, :] = h
        root[at, :] = jnp.broadcast_to(scale, (CHUNK, PAIR))
        normed[at, :] = (h * gain[...]).astype(BF16)
        ffn_grad[at, :] = jnp.where(valid(c), cot[at, :].astype(F32), 0.0).astype(BF16)
        return carry

    lax.fori_loop(0, total // CHUNK, mid_norm, 0)
    for n in range(0, 2 * hidden_units, 256):
        expanded[:, n : n + 256] = nn(normed[...], we[:, n : n + 256])

    def gate(c, carry):
        at = chunk_rows(c)
        for n in range(0, hidden_units, PAIR):
            a = expanded[at, n : n + PAIR]
            b = expanded[at, hidden_units + n : hidden_units + n + PAIR]
            phi = 0.5 + 0.5 * lax.erf(a * np.float32(0.5**0.5))
            density = np.float32((2 * np.pi) ** -0.5) * jnp.exp(a * a * -0.5)
            gelu = a * phi
            hid[at, n : n + PAIR] = (gelu * b).astype(BF16)
            expanded[at, n : n + PAIR] = b * (phi + a * density)
            expanded[at, hidden_units + n : hidden_units + n + PAIR] = gelu
        return carry

    lax.fori_loop(0, total // CHUNK, gate, 0)
    for n in range(0, width, 256):
        wide[:, n : n + 256] = nt(hid[...], wc[n : n + 256, :])

    def finish(c, carry):
        at = chunk_rows(c)
        result[at, :] = (mid[at, :] + jnp.where(valid(c), wide[at, :], 0.0)).astype(BF16)
        return carry

    lax.fori_loop(0, total // CHUNK, finish, 0)
    for n in range(0, hidden_units, 256):
        size = min(256, hidden_units - n)
        h = nn(ffn_grad[...], wc[:, n : n + size])
        exp_grad[:, n : n + size] = (h * expanded[:, n : n + size]).astype(BF16)
        exp_grad[:, hidden_units + n : hidden_units + n + size] = (
            h * expanded[:, hidden_units + n : hidden_units + n + size]
        ).astype(BF16)
    for n in range(0, width, 256):
        wide[:, n : n + 256] = nt(exp_grad[...], we[n : n + 256, :])

    def norm_back(c, carry):
        at = chunk_rows(c)
        g, h = wide[at, :], hat[at, :]
        gh = g * h
        mid_term[...] += jnp.sum(gh.reshape(CHUNK // 8, 8, width), axis=0)
        u = g * gain[...]
        mean_u = jnp.mean(u, axis=-1, keepdims=True)
        mean_uh = jnp.mean(u * h, axis=-1, keepdims=True)
        scale = jnp.concatenate([root[at, :]] * pairs, axis=1)
        m = cot[at, :].astype(F32) + (u - mean_u - h * mean_uh) * scale
        mid_grad[at, :] = m
        attn_grad[at, :] = jnp.where(valid(c), m, 0.0).astype(BF16)
        return carry

    lax.fori_loop(0, total // CHUNK, norm_back, 0)
    for n in range(0, width, 256):
        att_grad[:, n : n + 256] = nt(attn_grad[...], wp[n : n + 256, :]).astype(BF16)

    def attend_back(p, carry):
        lanes = pl.ds(pl.multiple_of(p * PAIR, PAIR), PAIR)
        for t in range(STEP_SLOTS):
            at = slice(t * rows, (t + 1) * rows)
            queries = two_heads(q[at, lanes] * jnp.asarray(HEAD_DIM**-0.5, BF16))
            grads = two_heads(att_grad[at, lanes])
            prob = probs[t, p]
            prob_grad = nt(vt[t, :, lanes], grads)
            total_grad = jnp.sum(prob * prob_grad, axis=0, keepdims=True)
            score_grad = (prob * (prob_grad - total_grad)).astype(BF16)
            tiles[1, t, :, lanes] = nn(prob.astype(BF16), grads)
            tiles[0, t, :, lanes] = nn(score_grad, queries)
            g = from_heads(tn(kt[t, :, lanes], score_grad), rows) * np.float32(HEAD_DIM**-0.5)
            c, s = slot_angles(slots[t][4], ca, sa, cb, sb)
            dq[at, lanes] = (g * c - swap_halves(g) * s).astype(BF16)
        return carry

    lax.fori_loop(0, pairs, attend_back, 0)
    for t, (slot, micro, pred, succ, _, _) in enumerate(slots):
        for which, out in ((0, dk), (1, dv)):
            part = which * half
            out[slot] += tiles[which, t, half : half + rows, :]

            @pl.when(pred < blocks)
            def _(out=out, which=which, t=t, micro=micro, pred=pred):
                out[micro * blocks + pred, half:, :] += tiles[which, t, :half, :]

            @pl.when(pred >= blocks)
            def _(part=part, which=which, t=t, micro=micro):
                back_prev[micro, part : part + half, :] = tiles[which, t, :half, :].astype(BF16)

            @pl.when(succ < blocks)
            def _(out=out, which=which, t=t, micro=micro, succ=succ):
                out[micro * blocks + succ, :half, :] += tiles[which, t, half + rows :, :]

            @pl.when(succ >= blocks)
            def _(part=part, which=which, t=t, micro=micro):
                back_next[micro, part : part + half, :] = tiles[which, t, half + rows :, :].astype(BF16)


def input_kernel(
    blocks, group, rows, width,
    lengths, dealing, dq, dk, dv, from_next, from_prev, x, mid_grad, w_all, gain, ca, sa, cb, sb,
    delta, input_grad, pre_term,
    w, wide, sem,
):
    step = pl.program_id(0)
    half = rows // 2

    @pl.when(step == 0)
    def _():
        copy = pltpu.make_async_copy(w_all.at[:, pl.ds(0, 3 * width)], w, sem)
        copy.start()
        copy.wait()
        pre_term[...] = jnp.zeros_like(pre_term)

    for t in range(STEP_SLOTS):
        micro, _, local, offset, _ = slot_scalars(lengths, dealing, step * STEP_SLOTS + t, blocks, group)
        c, s = slot_angles(offset, ca, sa, cb, sb)
        last = jnp.where(local == blocks - 1, 1.0, 0.0)
        first = jnp.where(local == 0, 1.0, 0.0)
        for top, weight, back in ((0, first, from_prev), (half, last, from_next)):
            at = slice(t * rows + top, t * rows + top + half)
            ct, st = c[top : top + half], s[top : top + half]
            for p in range(width // PAIR):
                lanes = slice(p * PAIR, (p + 1) * PAIR)
                g = dk[t, top : top + half, lanes] + weight * back[micro, :half, lanes].astype(F32)
                delta[at, lanes] = dq[at, lanes]
                delta[at, width + p * PAIR : width + (p + 1) * PAIR] = (g * ct - swap_halves(g) * st).astype(BF16)
                g = dv[t, top : top + half, lanes] + weight * back[micro, half:, lanes].astype(F32)
                delta[at, 2 * width + p * PAIR : 2 * width + (p + 1) * PAIR] = g.astype(BF16)
    for n in range(0, width, 256):
        wide[:, n : n + 256] = nt(delta[...], w[n : n + 256, :])

    def norm_back(c, carry):
        at = chunk_rows(c)
        xf = x[at, :].astype(F32)
        centred = xf - jnp.mean(xf, axis=-1, keepdims=True)
        spread = jnp.mean(centred * centred, axis=-1, keepdims=True)
        scale = lax.rsqrt(spread + norm_epsilon)
        h = centred * scale
        g = wide[at, :]
        pre_term[...] += jnp.sum((g * h).reshape(CHUNK // 8, 8, width), axis=0)
        u = g * gain[...]
        mean_u = jnp.mean(u, axis=-1, keepdims=True)
        mean_uh = jnp.mean(u * h, axis=-1, keepdims=True)
        input_grad[at, :] = (mid_grad[at, :] + (u - mean_u - h * mean_uh) * scale).astype(BF16)
        return carry

    lax.fori_loop(0, STEP_SLOTS * rows // CHUNK, norm_back, 0)


def shifted(block, axis, distance):
    devices = range(lax.axis_size(axis))
    route = [(i - distance, i) for i in devices if i - distance in devices]
    return lax.ppermute(block, axis, route)


def whole(shape):
    return pl.BlockSpec(shape, lambda i: (0,) * len(shape), pipeline_mode=pl.Buffered(1))


def by_step(shape):
    return pl.BlockSpec(shape, lambda i: (i,) + (0,) * (len(shape) - 1))


SMEM = pl.BlockSpec(memory_space=pltpu.SMEM)
ANY = pl.BlockSpec(memory_space=pl.ANY)


def local(
    inputs, cotangent, qkv_weight, proj_weight, expand_weight, contract_weight,
    prenorm, midnorm, lengths, dealing, holders, counts,
):
    micros, row_count, width = inputs.shape
    blocks = dealing.shape[1]
    rows = row_count // blocks
    hidden_units = contract_weight.shape[0]
    share = qkv_weight.shape[0]
    group = blocks * lax.axis_size("fsdp")
    slots = micros * blocks
    steps = slots // STEP_SLOTS
    total = slots * rows
    per = STEP_SLOTS * rows
    axes = ("dp", "fsdp")
    sds = jax.ShapeDtypeStruct
    tables = rope_tables(group, rows)
    table_specs = [whole(t.shape) for t in tables]
    lengths = lengths.reshape(micros, -1)
    holders = holders.reshape(micros * 2, blocks)
    x = inputs.reshape(total, width)
    cot = cotangent.reshape(total, width)

    gains = jnp.pad(jnp.stack([prenorm, midnorm], axis=1), ((0, 0), (0, PAIR - 2)))
    packed = jnp.concatenate([qkv_weight, expand_weight, contract_weight.T, proj_weight, gains], axis=1)
    w_all = lax.all_gather(packed, axes, axis=0, tiled=True)
    columns = w_all.shape[1]
    gains = w_all[:, columns - PAIR : columns - PAIR + 2].astype(F32).T
    gain_pre, gain_mid = gains[0:1], gains[1:2]
    params = functools.partial(pltpu.CompilerParams, vmem_limit_bytes=VMEM_LIMIT, dimension_semantics=("arbitrary",))

    q, k, v, normed_one, to_next, to_prev = pl.pallas_call(
        functools.partial(qkv_kernel, blocks, group, rows, width),
        grid=(steps,),
        in_specs=[SMEM] * 3 + [by_step((per, width)), ANY, whole((1, width))] + table_specs,
        out_specs=[by_step((per, width))] * 4 + [whole((micros, rows, width)), whole((micros, rows + 16, width))],
        out_shape=[sds((total, width), BF16)] * 4
        + [sds((micros, rows, width), BF16), sds((micros, rows + 16, width), BF16)],
        scratch_shapes=[
            pltpu.VMEM((width, 3 * width), BF16),
            pltpu.VMEM((per, 3 * width), F32),
            pltpu.VMEM((per, PAIR), F32),
            pltpu.VMEM((per, PAIR), F32),
            pltpu.SemaphoreType.DMA,
        ],
        compiler_params=params(),
        name="qkv",
    )(lengths, dealing, counts, x, w_all, gain_pre, *tables)

    from_prev = shifted(to_next, "fsdp", 1)
    from_next = shifted(to_prev, "fsdp", -1)

    outs = pl.pallas_call(
        functools.partial(layer_kernel, blocks, group, rows, width, hidden_units),
        grid=(steps,),
        in_specs=[SMEM] * 4
        + [by_step((per, width)), whole((slots, rows, width)), whole((slots, rows, width))]
        + [whole((micros, rows, width)), whole((micros, rows + 16, width))]
        + [by_step((per, width))] * 2
        + [ANY, whole((1, width))]
        + table_specs,
        out_specs=[by_step((per, width))] * 3
        + [by_step((per, hidden_units)), by_step((per, width)), by_step((per, width))]
        + [by_step((per, 2 * hidden_units)), by_step((per, width)), by_step((per, width))]
        + [whole((slots, rows, width))] * 2
        + [whole((micros, rows, width))] * 2
        + [whole((8, width))],
        out_shape=[
            sds((total, width), BF16),
            sds((total, width), F32),
            sds((total, width), BF16),
            sds((total, hidden_units), BF16),
            sds((total, width), BF16),
            sds((total, width), BF16),
            sds((total, 2 * hidden_units), BF16),
            sds((total, width), BF16),
            sds((total, width), BF16),
            sds((slots, rows, width), F32),
            sds((slots, rows, width), F32),
            sds((micros, rows, width), BF16),
            sds((micros, rows, width), BF16),
            sds((8, width), F32),
        ],
        scratch_shapes=[
            pltpu.VMEM((width, width), BF16),
            pltpu.VMEM((width, 2 * hidden_units), BF16),
            pltpu.VMEM((width, hidden_units), BF16),
            pltpu.VMEM((STEP_SLOTS, 2 * rows, width), BF16),
            pltpu.VMEM((STEP_SLOTS, 2 * rows, width), BF16),
            pltpu.VMEM((STEP_SLOTS, 2 * rows, rows), F32),
            pltpu.VMEM((STEP_SLOTS, width // PAIR, 2 * rows, 2 * rows), F32),
            pltpu.VMEM((per, 2 * hidden_units), F32),
            pltpu.VMEM((per, width), F32),
            pltpu.VMEM((per, width), F32),
            pltpu.VMEM((per, width), F32),
            pltpu.VMEM((per, PAIR), F32),
            pltpu.VMEM((per, width), BF16),
            pltpu.VMEM((2, STEP_SLOTS, 2 * rows, width), F32),
            pltpu.SemaphoreType.DMA((3,)),
        ],
        compiler_params=params(),
        name="layer",
    )(
        lengths, dealing, holders, counts,
        q, k.reshape(slots, rows, width), v.reshape(slots, rows, width),
        from_prev, from_next, x, cot, w_all, gain_mid, *tables,
    )
    result, mid_grad, dq, hid, ffn_grad, normed_two, exp_grad, attended, attn_grad = outs[:9]
    dk, dv, back_prev, back_next, mid_term = outs[9:]

    ret_next = shifted(back_prev, "fsdp", -1)
    ret_prev = shifted(back_next, "fsdp", 1)
    term_expand = tn(normed_two, exp_grad).astype(BF16)
    term_contract = tn(ffn_grad, hid).astype(BF16)
    term_proj = tn(attended, attn_grad).astype(BF16)

    delta, input_grad, pre_term = pl.pallas_call(
        functools.partial(input_kernel, blocks, group, rows, width),
        grid=(steps,),
        in_specs=[SMEM] * 2
        + [by_step((per, width)), by_step((STEP_SLOTS, rows, width)), by_step((STEP_SLOTS, rows, width))]
        + [whole((micros, rows, width))] * 2
        + [by_step((per, width))] * 2
        + [ANY, whole((1, width))]
        + table_specs,
        out_specs=[by_step((per, 3 * width)), by_step((per, width)), whole((8, width))],
        out_shape=[sds((total, 3 * width), BF16), sds((total, width), BF16), sds((8, width), F32)],
        scratch_shapes=[
            pltpu.VMEM((width, 3 * width), BF16),
            pltpu.VMEM((per, width), F32),
            pltpu.SemaphoreType.DMA,
        ],
        compiler_params=params(),
        name="input",
    )(lengths, dealing, dq, dk, dv, ret_next, ret_prev, x, mid_grad, w_all, gain_pre, *tables)
    term_qkv = tn(normed_one, delta).astype(BF16)

    terms = jnp.stack([jnp.sum(pre_term, axis=0), jnp.sum(mid_term, axis=0)], axis=1)
    terms = jnp.pad(terms, ((0, 0), (0, PAIR - 2))).astype(BF16)
    grads = jnp.concatenate([term_qkv, term_expand, term_contract, term_proj, terms], axis=1)
    shard = lax.psum_scatter(grads, axes, scatter_dimension=0, tiled=True).astype(F32)
    at = np.cumsum([0, 3 * width, 2 * hidden_units, hidden_units, width])
    return (
        result.reshape(inputs.shape),
        input_grad.reshape(inputs.shape),
        shard[:, at[0] : at[1]],
        shard[:, at[3] : at[4]],
        shard[:, at[1] : at[2]],
        shard[:, at[2] : at[3]].T,
        shard[:, at[4]],
        shard[:, at[4] + 1],
    )


def solution(mesh):
    both = ("dp", "fsdp")
    return jax.shard_map(
        local,
        mesh=mesh,
        in_specs=(
            P(None, both, None), P(None, both, None),
            P(both, None), P(both, None), P(both, None), P(None, both), P(both), P(both),
            P(None, "dp", None), P(None, both), P(None, None, both), P(None, both),
        ),
        out_specs=(
            P(None, both, None), P(None, both, None),
            P(both, None), P(both, None), P(both, None), P(None, both), P(both), P(both),
        ),
        check_vma=False,
    )
```

```python
import functools

import jax
import jax.numpy as jnp
import numpy as np
from jax import lax
from jax.experimental import pallas as pl
from jax.experimental.pallas import tpu as pltpu
from jax.sharding import PartitionSpec as P

HEAD_DIM = 64
PAIR = 128
STEP_SLOTS = 2
CHUNK = 32
norm_epsilon = 1e-05
rope_base = 10000.0
masked_score = -1e30
F32 = jnp.float32
BF16 = jnp.bfloat16
VMEM_LIMIT = 60 * 1024 * 1024


def nn(a, b):
    return lax.dot_general(a, b, (((1,), (0,)), ((), ())), preferred_element_type=F32)


def nt(a, b):
    return lax.dot_general(a, b, (((1,), (1,)), ((), ())), preferred_element_type=F32)


def tn(a, b):
    return lax.dot_general(a, b, (((0,), (0,)), ((), ())), preferred_element_type=F32)


def rope_tables(most_offset, block_rows):
    half = HEAD_DIM // 2
    freq = rope_base ** (-np.arange(half) * (2.0 / HEAD_DIM))
    freq = np.tile(freq, PAIR // half)
    sign = np.where(np.arange(PAIR) % HEAD_DIM < half, -1.0, 1.0)

    def pair(positions):
        angles = positions[:, None] * freq[None, :]
        return (
            jnp.asarray(np.cos(angles), F32),
            jnp.asarray(np.sin(angles) * sign[None, :], F32),
        )

    return (*pair(np.arange(most_offset) * float(block_rows)), *pair(np.arange(block_rows) * 1.0))


def slot_scalars(lengths, dealing, slot, blocks, group):
    micro = slot // blocks
    place = slot - micro * blocks
    block = dealing[micro, place]
    within = lax.rem(block, group)
    begin = jnp.int32(0)
    start = jnp.int32(0)
    ends = jnp.int32(0)
    for seq in range(lengths.shape[1]):
        begin = jnp.where(start <= within, start, begin)
        start = start + lengths[micro, seq]
        ends = ends + jnp.where(start - 1 == within, 1, 0)
    return micro, place, lax.rem(block, blocks), within - begin, ends > 0


def slot_angles(offset, ca, sa, cb, sb):
    first_c, first_s = ca[pl.ds(offset, 1), :], sa[pl.ds(offset, 1), :]
    return first_c * cb[...] - first_s * sb[...], first_s * cb[...] + first_c * sb[...]


def swap_halves(v):
    low = lax.broadcasted_iota(jnp.int32, v.shape, 1) % HEAD_DIM < HEAD_DIM // 2
    return jnp.where(low, pltpu.roll(v, PAIR - HEAD_DIM // 2, 1), pltpu.roll(v, HEAD_DIM // 2, 1))


def head_masks(dtype):
    low = lax.broadcasted_iota(jnp.int32, (1, PAIR), 1) < HEAD_DIM
    return low.astype(F32).astype(dtype), (1.0 - low.astype(F32)).astype(dtype)


def two_heads(tile):
    even, odd = head_masks(tile.dtype)
    return jnp.concatenate([tile * even, tile * odd], axis=0)


def from_heads(t, rows):
    return jnp.concatenate([t[:HEAD_DIM, :rows], t[HEAD_DIM:, rows:]], axis=0).T


def chunk_rows(c, size=CHUNK):
    return pl.ds(pl.multiple_of(c * size, size), size)


def qkv_kernel(
    blocks, group, rows, width,
    lengths, dealing, counts, x, w_all, gain, ca, sa, cb, sb,
    q, k, v, normed, to_next, to_prev,
    w, full, cos, sin, sem,
):
    step = pl.program_id(0)
    half = rows // 2

    @pl.when(step == 0)
    def _():
        copy = pltpu.make_async_copy(w_all.at[:, pl.ds(0, 3 * width)], w, sem)
        copy.start()
        copy.wait()

    slots = [slot_scalars(lengths, dealing, step * STEP_SLOTS + t, blocks, group) for t in range(STEP_SLOTS)]
    for t, (_, _, _, offset, _) in enumerate(slots):
        c, s = slot_angles(offset, ca, sa, cb, sb)
        cos[t * rows : (t + 1) * rows, :] = c
        sin[t * rows : (t + 1) * rows, :] = s

    def norm(c, carry):
        at = chunk_rows(c)
        xf = x[at, :].astype(F32)
        centred = xf - jnp.mean(xf, axis=-1, keepdims=True)
        spread = jnp.mean(centred * centred, axis=-1, keepdims=True)
        normed[at, :] = (centred * lax.rsqrt(spread + norm_epsilon) * gain[...]).astype(BF16)
        return carry

    lax.fori_loop(0, STEP_SLOTS * rows // CHUNK, norm, 0)
    for n in range(0, 3 * width, 256):
        full[:, n : n + 256] = nn(normed[...], w[:, n : n + 256])

    def turn(c, carry):
        at = chunk_rows(c)
        co, si = cos[at, :], sin[at, :]
        for p in range(width // PAIR):
            lanes = slice(p * PAIR, (p + 1) * PAIR)
            for out, base in ((q, 0), (k, width)):
                tile = full[at, base + p * PAIR : base + (p + 1) * PAIR]
                out[at, lanes] = (tile * co + swap_halves(tile) * si).astype(BF16)
            v[at, lanes] = full[at, 2 * width + p * PAIR : 2 * width + (p + 1) * PAIR].astype(BF16)
        return carry

    lax.fori_loop(0, STEP_SLOTS * rows // CHUNK, turn, 0)
    for t, (micro, _, local, _, _) in enumerate(slots):
        base = t * rows

        @pl.when(local == blocks - 1)
        def _(micro=micro, base=base):
            to_next[micro, :half, :] = k[base + half : base + rows, :]
            to_next[micro, half:, :] = v[base + half : base + rows, :]

        @pl.when(local == 0)
        def _(micro=micro, base=base):
            to_prev[micro, :half, :] = k[base : base + half, :]
            to_prev[micro, half:rows, :] = v[base : base + half, :]
            valid = jnp.full((16, width), counts[micro, 0], jnp.int32).astype(F32)
            to_prev[micro, rows:, :] = valid.astype(BF16)


def layer_kernel(
    blocks, group, rows, width, hidden_units,
    lengths, dealing, holders, counts,
    q, k, v, from_prev, from_next, x, cot, w_all, gain, ca, sa, cb, sb,
    result, mid_grad, dq, hid, ffn_grad, normed, exp_grad, attended, attn_grad,
    dk, dv, back_prev, back_next, mid_term,
    wp, we, wc, kt, vt, bias, probs, expanded, wide, mid, hat, root, att_grad, tiles, sem,
):
    step = pl.program_id(0)
    half = rows // 2
    total = STEP_SLOTS * rows
    pairs = width // PAIR

    def weights():
        at = 3 * width
        out = []
        for place, (dst, cols) in enumerate(((we, 2 * hidden_units), (wc, hidden_units), (wp, width))):
            out.append(pltpu.make_async_copy(w_all.at[:, pl.ds(at, cols)], dst, sem.at[place]))
            at += cols
        return out

    @pl.when(step == 0)
    def _():
        for copy in weights():
            copy.start()
        dk[...] = jnp.zeros_like(dk)
        dv[...] = jnp.zeros_like(dv)
        mid_term[...] = jnp.zeros_like(mid_term)

    slots = []
    for t in range(STEP_SLOTS):
        slot = step * STEP_SLOTS + t
        micro, place, local, offset, is_last = slot_scalars(lengths, dealing, slot, blocks, group)
        pred, succ = holders[micro * 2, place], holders[micro * 2 + 1, place]
        count = counts[micro, local]
        slots.append((slot, micro, pred, succ, offset, count))
        for src, dst, part in ((k, kt, 0), (v, vt, half)):
            @pl.when(pred < blocks)
            def _(src=src, dst=dst, t=t, micro=micro, pred=pred):
                dst[t, :half, :] = src[micro * blocks + pred, half:, :]

            @pl.when(pred >= blocks)
            def _(dst=dst, part=part, t=t, micro=micro):
                dst[t, :half, :] = from_prev[micro, part : part + half, :]

            dst[t, half : half + rows, :] = src[slot]

            @pl.when(succ < blocks)
            def _(src=src, dst=dst, t=t, micro=micro, succ=succ):
                dst[t, half + rows :, :] = src[micro * blocks + succ, :half, :]

            @pl.when(succ >= blocks)
            def _(dst=dst, part=part, t=t, micro=micro):
                dst[t, half + rows :, :] = from_next[micro, part : part + half, :]

        col = lax.broadcasted_iota(jnp.int32, (2 * rows, rows), 0)
        row = lax.broadcasted_iota(jnp.int32, (2 * rows, rows), 1)
        follow = counts[micro, lax.rem(local + 1, blocks)]
        remote = from_next[micro, rows : rows + 1, :rows].astype(F32)
        follow = jnp.where(succ < blocks, jnp.full((1, rows), follow, jnp.int32).astype(F32), remote)
        follow = half + rows + jnp.minimum(follow, half)
        ends = jnp.full((1, rows), half + count, jnp.int32).astype(F32)
        high = jnp.where(is_last, ends, follow)
        lowest = jnp.where(offset > 0, 0, half)
        allowed = (col >= row) & (col - row <= rows) & (col >= lowest) & (col.astype(F32) < high)
        bias[t] = jnp.where(allowed, 0.0, masked_score)

    def attend(p, carry):
        lanes = pl.ds(pl.multiple_of(p * PAIR, PAIR), PAIR)
        for t in range(STEP_SLOTS):
            at = slice(t * rows, (t + 1) * rows)
            queries = two_heads(q[at, lanes] * jnp.asarray(HEAD_DIM**-0.5, BF16))
            scores = nt(kt[t, :, lanes], queries)
            scores = scores + jnp.concatenate([bias[t], bias[t]], axis=1)
            lifted = jnp.exp(scores - jnp.max(scores, axis=0, keepdims=True))
            prob = lifted * (1.0 / jnp.sum(lifted, axis=0, keepdims=True))
            probs[t, p] = prob
            mixed = tn(vt[t, :, lanes], prob.astype(BF16))
            attended[at, lanes] = from_heads(mixed, rows).astype(BF16)
        return carry

    lax.fori_loop(0, pairs, attend, 0)

    @pl.when(step == 0)
    def _():
        for copy in weights():
            copy.wait()

    def valid(c):
        per = rows // CHUNK
        inside = lax.rem(c, per) * CHUNK
        count = jnp.where(c < per, slots[0][5], slots[1][5])
        r = lax.broadcasted_iota(jnp.int32, (CHUNK, width), 0) + inside
        return r < count

    for n in range(0, width, 256):
        wide[:, n : n + 256] = nn(attended[...], wp[:, n : n + 256])

    def mid_norm(c, carry):
        at = chunk_rows(c)
        m = x[at, :].astype(F32) + jnp.where(valid(c), wide[at, :], 0.0)
        mid[at, :] = m
        centred = m - jnp.mean(m, axis=-1, keepdims=True)
        spread = jnp.mean(centred * centred, axis=-1, keepdims=True)
        scale = lax.rsqrt(spread + norm_epsilon)
        h = centred * scale
        hat[at, :] = h
        root[at, :] = jnp.broadcast_to(scale, (CHUNK, PAIR))
        normed[at, :] = (h * gain[...]).astype(BF16)
        ffn_grad[at, :] = jnp.where(valid(c), cot[at, :].astype(F32), 0.0).astype(BF16)
        return carry

    lax.fori_loop(0, total // CHUNK, mid_norm, 0)
    for n in range(0, 2 * hidden_units, 256):
        expanded[:, n : n + 256] = nn(normed[...], we[:, n : n + 256])

    def gate(c, carry):
        at = chunk_rows(c)
        for n in range(0, hidden_units, PAIR):
            a = expanded[at, n : n + PAIR]
            b = expanded[at, hidden_units + n : hidden_units + n + PAIR]
            phi = 0.5 + 0.5 * lax.erf(a * np.float32(0.5**0.5))
            density = np.float32((2 * np.pi) ** -0.5) * jnp.exp(a * a * -0.5)
            gelu = a * phi
            hid[at, n : n + PAIR] = (gelu * b).astype(BF16)
            expanded[at, n : n + PAIR] = b * (phi + a * density)
            expanded[at, hidden_units + n : hidden_units + n + PAIR] = gelu
        return carry

    lax.fori_loop(0, total // CHUNK, gate, 0)
    for n in range(0, width, 256):
        wide[:, n : n + 256] = nt(hid[...], wc[n : n + 256, :])

    def finish(c, carry):
        at = chunk_rows(c)
        result[at, :] = (mid[at, :] + jnp.where(valid(c), wide[at, :], 0.0)).astype(BF16)
        return carry

    lax.fori_loop(0, total // CHUNK, finish, 0)
    for n in range(0, hidden_units, 256):
        size = min(256, hidden_units - n)
        h = nn(ffn_grad[...], wc[:, n : n + size])
        exp_grad[:, n : n + size] = (h * expanded[:, n : n + size]).astype(BF16)
        exp_grad[:, hidden_units + n : hidden_units + n + size] = (
            h * expanded[:, hidden_units + n : hidden_units + n + size]
        ).astype(BF16)
    for n in range(0, width, 256):
        wide[:, n : n + 256] = nt(exp_grad[...], we[n : n + 256, :])

    def norm_back(c, carry):
        at = chunk_rows(c)
        g, h = wide[at, :], hat[at, :]
        gh = g * h
        mid_term[...] += jnp.sum(gh.reshape(CHUNK // 8, 8, width), axis=0)
        u = g * gain[...]
        mean_u = jnp.mean(u, axis=-1, keepdims=True)
        mean_uh = jnp.mean(u * h, axis=-1, keepdims=True)
        scale = jnp.concatenate([root[at, :]] * pairs, axis=1)
        m = cot[at, :].astype(F32) + (u - mean_u - h * mean_uh) * scale
        mid_grad[at, :] = m
        attn_grad[at, :] = jnp.where(valid(c), m, 0.0).astype(BF16)
        return carry

    lax.fori_loop(0, total // CHUNK, norm_back, 0)
    for n in range(0, width, 256):
        att_grad[:, n : n + 256] = nt(attn_grad[...], wp[n : n + 256, :]).astype(BF16)

    def attend_back(p, carry):
        lanes = pl.ds(pl.multiple_of(p * PAIR, PAIR), PAIR)
        for t in range(STEP_SLOTS):
            at = slice(t * rows, (t + 1) * rows)
            queries = two_heads(q[at, lanes] * jnp.asarray(HEAD_DIM**-0.5, BF16))
            grads = two_heads(att_grad[at, lanes])
            prob = probs[t, p]
            prob_grad = nt(vt[t, :, lanes], grads)
            total_grad = jnp.sum(prob * prob_grad, axis=0, keepdims=True)
            score_grad = (prob * (prob_grad - total_grad)).astype(BF16)
            tiles[1, t, :, lanes] = nn(prob.astype(BF16), grads)
            tiles[0, t, :, lanes] = nn(score_grad, queries)
            g = from_heads(tn(kt[t, :, lanes], score_grad), rows) * np.float32(HEAD_DIM**-0.5)
            c, s = slot_angles(slots[t][4], ca, sa, cb, sb)
            dq[at, lanes] = (g * c - swap_halves(g) * s).astype(BF16)
        return carry

    lax.fori_loop(0, pairs, attend_back, 0)
    for t, (slot, micro, pred, succ, _, _) in enumerate(slots):
        for which, out in ((0, dk), (1, dv)):
            part = which * half
            out[slot] += tiles[which, t, half : half + rows, :]

            @pl.when(pred < blocks)
            def _(out=out, which=which, t=t, micro=micro, pred=pred):
                out[micro * blocks + pred, half:, :] += tiles[which, t, :half, :]

            @pl.when(pred >= blocks)
            def _(part=part, which=which, t=t, micro=micro):
                back_prev[micro, part : part + half, :] = tiles[which, t, :half, :].astype(BF16)

            @pl.when(succ < blocks)
            def _(out=out, which=which, t=t, micro=micro, succ=succ):
                out[micro * blocks + succ, :half, :] += tiles[which, t, half + rows :, :]

            @pl.when(succ >= blocks)
            def _(part=part, which=which, t=t, micro=micro):
                back_next[micro, part : part + half, :] = tiles[which, t, half + rows :, :].astype(BF16)


def input_kernel(
    blocks, group, rows, width,
    lengths, dealing, dq, dk, dv, from_next, from_prev, x, mid_grad, w_all, gain, ca, sa, cb, sb,
    delta, input_grad, pre_term,
    w, wide, sem,
):
    step = pl.program_id(0)
    half = rows // 2

    @pl.when(step == 0)
    def _():
        copy = pltpu.make_async_copy(w_all.at[:, pl.ds(0, 3 * width)], w, sem)
        copy.start()
        copy.wait()
        pre_term[...] = jnp.zeros_like(pre_term)

    for t in range(STEP_SLOTS):
        micro, _, local, offset, _ = slot_scalars(lengths, dealing, step * STEP_SLOTS + t, blocks, group)
        c, s = slot_angles(offset, ca, sa, cb, sb)
        last = jnp.where(local == blocks - 1, 1.0, 0.0)
        first = jnp.where(local == 0, 1.0, 0.0)
        for top, weight, back in ((0, first, from_prev), (half, last, from_next)):
            at = slice(t * rows + top, t * rows + top + half)
            ct, st = c[top : top + half], s[top : top + half]
            for p in range(width // PAIR):
                lanes = slice(p * PAIR, (p + 1) * PAIR)
                g = dk[t, top : top + half, lanes] + weight * back[micro, :half, lanes].astype(F32)
                delta[at, lanes] = dq[at, lanes]
                delta[at, width + p * PAIR : width + (p + 1) * PAIR] = (g * ct - swap_halves(g) * st).astype(BF16)
                g = dv[t, top : top + half, lanes] + weight * back[micro, half:, lanes].astype(F32)
                delta[at, 2 * width + p * PAIR : 2 * width + (p + 1) * PAIR] = g.astype(BF16)
    for n in range(0, width, 256):
        wide[:, n : n + 256] = nt(delta[...], w[n : n + 256, :])

    def norm_back(c, carry):
        at = chunk_rows(c)
        xf = x[at, :].astype(F32)
        centred = xf - jnp.mean(xf, axis=-1, keepdims=True)
        spread = jnp.mean(centred * centred, axis=-1, keepdims=True)
        scale = lax.rsqrt(spread + norm_epsilon)
        h = centred * scale
        g = wide[at, :]
        pre_term[...] += jnp.sum((g * h).reshape(CHUNK // 8, 8, width), axis=0)
        u = g * gain[...]
        mean_u = jnp.mean(u, axis=-1, keepdims=True)
        mean_uh = jnp.mean(u * h, axis=-1, keepdims=True)
        input_grad[at, :] = (mid_grad[at, :] + (u - mean_u - h * mean_uh) * scale).astype(BF16)
        return carry

    lax.fori_loop(0, STEP_SLOTS * rows // CHUNK, norm_back, 0)


def shifted(block, axis, distance):
    devices = range(lax.axis_size(axis))
    route = [(i - distance, i) for i in devices if i - distance in devices]
    return lax.ppermute(block, axis, route)


def whole(shape):
    return pl.BlockSpec(shape, lambda i: (0,) * len(shape), pipeline_mode=pl.Buffered(1))


def by_step(shape):
    return pl.BlockSpec(shape, lambda i: (i,) + (0,) * (len(shape) - 1))


SMEM = pl.BlockSpec(memory_space=pltpu.SMEM)
ANY = pl.BlockSpec(memory_space=pl.ANY)


MESH = pl.DeviceIdType.MESH
LANES = 512


class Place:
    def __init__(self):
        self.nz, self.fs = lax.axis_size("dp"), lax.axis_size("fsdp")
        self.z = lax.axis_index("dp")
        self.f = lax.axis_index("fsdp")
        self.c = lax.rem(self.f, 2)
        first, second = self.f // 4, lax.rem(self.f // 2, 2)
        self.a2 = self.c * second + (1 - self.c) * first
        self.a3 = self.c * first + (1 - self.c) * second
        self.s2 = 4 - 2 * self.c
        self.s3 = 2 + 2 * self.c

    def square(self, x2, x3):
        return x2 * self.s2 + x3 * self.s3

    def at(self, z=None, x2=None, x3=None, other=False):
        z = self.z if z is None else z
        x2 = self.a2 if x2 is None else x2
        x3 = self.a3 if x3 is None else x3
        c = 1 - self.c if other else self.c
        return {"dp": z, "fsdp": self.square(x2, x3) + c}

    def greet(self):
        barrier = pltpu.get_barrier_semaphore()
        last = self.nz - 1

        def signal(device):
            pl.semaphore_signal(barrier, inc=1, device_id=device, device_id_type=MESH)

        signal(self.at(x2=1 - self.a2))
        signal(self.at(x3=1 - self.a3))
        signal(self.at(other=True))
        pl.when(self.z < last)(lambda: signal(self.at(z=self.z + 1)))
        pl.when(self.z > 0)(lambda: signal(self.at(z=self.z - 1)))
        pl.semaphore_wait(barrier, 3 + (self.z + last) // self.nz + (2 * last - self.z) // self.nz)


def gather_kernel(own, out, send, recv, local_sem):
    at = Place()
    z, nz, c = at.z, at.nz, at.c
    at.greet()
    started = []

    def item(zz, x2, x3, core):
        return zz * at.fs + at.square(x2, x3) + core

    def copy(src, it, slot, device):
        return pltpu.make_async_remote_copy(
            src_ref=src, dst_ref=out.at[it], send_sem=send.at[slot, it], recv_sem=recv.at[it],
            device_id=device, device_id_type=MESH,
        )

    def arrived(it):
        copy(out.at[it], it, 0, at.at(other=True)).wait_recv()

    def guarded(cond, fn):
        if cond is None:
            fn()
        else:
            pl.when(cond)(fn)

    def handle(it, src, cond, targets):
        def body():
            if cond is not True:
                arrived(it)
            for slot, device, inner in targets:
                guarded(inner, lambda: copy(src(), it, slot, device).start())

        guarded(None if cond is True else cond, body)
        for slot, device, inner in targets:
            parts = [p for p in (cond, inner) if p is not None and p is not True]
            both = functools.reduce(jnp.logical_and, parts) if parts else None
            started.append((it, slot, device, both))

    up = (0, at.at(z=z + 1), z < nz - 1)
    down = (1, at.at(z=z - 1), z > 0)
    over2 = (2, at.at(x2=1 - at.a2), None)
    over3 = (3, at.at(x3=1 - at.a3), None)
    over = (4, at.at(other=True), None)
    a2, a3 = at.a2, at.a3
    mine = item(z, a2, a3, c)
    handle(mine, lambda: own, True, (over3, over2, up, down, over))
    keep = pltpu.make_async_copy(own, out.at[mine], local_sem)
    keep.start()

    def forward(zz, x2, x3, cond, targets):
        it = item(zz, x2, x3, c)
        handle(it, lambda: out.at[it], cond, targets)

    def third(zz, cond):
        for x2 in (a2, 1 - a2):
            forward(zz, x2, 1 - a3, cond, (over,))

    sources = [(z, None, None)]
    for d in range(1, nz):
        sources.append((z - d, z - d >= 0, up))
        sources.append((z + d, z + d < nz, down))
    for n, (zz, cond, ahead) in enumerate(sources):
        if ahead is not None:
            forward(zz, a2, a3, cond, (over3, over2, ahead, over))
        forward(zz, 1 - a2, a3, cond, (over3, over))
        if n >= 1:
            third(*sources[n - 1][:2])
    third(*sources[-1][:2])

    def other(n, carry):
        arrived(2 * n + 1 - c)
        return carry

    lax.fori_loop(0, nz * at.fs // 2, other, 0)
    keep.wait()
    for it, slot, device, cond in started:
        guarded(cond, lambda: copy(out.at[it], it, slot, device).wait_send())


def gather(packed):
    nz, fs = lax.axis_size("dp"), lax.axis_size("fsdp")
    if fs != 8 or packed.shape[0] % 8:
        return lax.all_gather(packed, ("dp", "fsdp"), axis=0, tiled=True)
    devices = nz * fs
    out = pl.pallas_call(
        gather_kernel,
        in_specs=[pl.BlockSpec(memory_space=pltpu.VMEM)],
        out_specs=ANY,
        out_shape=jax.ShapeDtypeStruct((devices, *packed.shape), packed.dtype),
        scratch_shapes=[
            pltpu.SemaphoreType.DMA((5, devices)),
            pltpu.SemaphoreType.DMA((devices,)),
            pltpu.SemaphoreType.DMA,
        ],
        compiler_params=pltpu.CompilerParams(collective_id=0, has_side_effects=True),
        name="gather",
    )(packed)
    return out.reshape(-1, packed.shape[1])


def reduce_kernel(
    grads, out,
    own, side, over3, over2, from_below, from_above,
    own_sem, side_send, side_recv, send3, recv3, send2, recv2, send_up, recv_up, send_down, recv_down,
):
    at = Place()
    z, nz, c, a2, a3 = at.z, at.nz, at.c, at.a2, at.a3
    share, columns = out.shape
    squares = at.fs // 2
    at.greet()

    def remote(src, dst, send, recv, device):
        return pltpu.make_async_remote_copy(
            src_ref=src, dst_ref=dst, send_sem=send, recv_sem=recv, device_id=device, device_id_type=MESH
        )

    def item(zz, x2, x3):
        return zz * squares + at.square(x2, x3) // 2

    sign = 1 - 2 * (z // (nz // 2))
    order = [lax.rem(z + sign * o + nz, nz) for o in range(nz - 1, -1, -1)]

    def partner_copy(i):
        return remote(grads.at[i, 1 - c], side.at[i], side_send.at[i], side_recv.at[i], at.at(other=True))

    keep = pltpu.make_async_copy(grads.at[:, c], own, own_sem)
    keep.start()
    for far in (1 - a2, a2):
        for zz in order:
            for x3 in (1 - a3, a3):
                partner_copy(item(zz, far, x3)).start()
    keep.wait()

    def add(i, *terms):
        def some(n, carry):
            lanes = pl.ds(pl.multiple_of(n * LANES, LANES), LANES)
            value = own[i, :, lanes].astype(F32)
            for ref, j in terms:
                value = value + ref[j, :, lanes].astype(F32)
            own[i, :, lanes] = value.astype(BF16)
            return carry

        lax.fori_loop(0, columns // LANES, some, 0)

    def copy3(i, slot):
        return remote(own.at[i], over3.at[slot], send3.at[slot], recv3.at[slot], at.at(x3=1 - a3))

    def copy2(i, k):
        return remote(own.at[i], over2.at[k], send2.at[k], recv2.at[k], at.at(x2=1 - a2))

    def copy_up(i, t):
        return remote(own.at[i], from_below.at[t], send_up.at[t], recv_up.at[t], at.at(z=z + 1))

    def copy_down(i, t):
        return remote(own.at[i], from_above.at[t], send_down.at[t], recv_down.at[t], at.at(z=z - 1))

    sent = []
    for k, zz in enumerate(order):
        for flag, x2 in ((1, 1 - a2), (0, a2)):
            i = item(zz, x2, 1 - a3)
            partner_copy(i).wait_recv()
            add(i, (side, i))
            one = copy3(i, 2 * k + flag)
            one.start()
            sent.append(one)

    def third(k):
        i = item(order[k], a2, a3)
        copy2(i, k).wait_recv()
        add(i, (over2, k))
        if k < nz - 1:
            pl.when(z == 0)(copy_up(i, order[k]).start)
            pl.when(z == nz - 1)(copy_down(i, order[k]).start)

    for k, zz in enumerate(order):
        for flag, x2 in ((1, 1 - a2), (0, a2)):
            i = item(zz, x2, a3)
            partner_copy(i).wait_recv()
            copy3(i, 2 * k + flag).wait_recv()
            add(i, (side, i), (over3, 2 * k + flag))
            if flag:
                one = copy2(i, k)
                one.start()
                sent.append(one)
        if k:
            third(k - 1)
    third(nz - 1)

    def climb(t):
        i = item(t, a2, a3)
        copy_up(i, t).wait_recv()
        add(i, (from_below, t))
        copy_up(i, t).start()

    def descend(t):
        i = item(t, a2, a3)
        copy_down(i, t).wait_recv()
        add(i, (from_above, t))
        copy_down(i, t).start()

    for zz in range(1, nz - 1):

        @pl.when(z == zz)
        def _(zz=zz):
            ups = [functools.partial(climb, t) for t in range(nz - 1, zz, -1)]
            downs = [functools.partial(descend, t) for t in range(zz)]
            for step in ups + downs if zz < nz // 2 else downs + ups:
                step()

    i = item(z, a2, a3)
    out[...] = own[i].astype(F32)

    @pl.when(z > 0)
    def _():
        copy_up(i, z).wait_recv()
        out[...] += from_below[z].astype(F32)

    @pl.when(z < nz - 1)
    def _():
        copy_down(i, z).wait_recv()
        out[...] += from_above[z].astype(F32)

    for one in sent:
        one.wait_send()
    for zz in range(nz):

        @pl.when(z == zz)
        def _(zz=zz):
            for t in range(zz + 1, nz):
                copy_up(item(t, a2, a3), t).wait_send()
            for t in range(zz):
                copy_down(item(t, a2, a3), t).wait_send()

    def partner_done(i, carry):
        partner_copy(i).wait_send()
        return carry

    lax.fori_loop(0, nz * squares, partner_done, 0)


def reduce_scatter(grads, share):
    nz, fs = lax.axis_size("dp"), lax.axis_size("fsdp")
    if fs != 8 or share % 8 or nz % 2:
        return lax.psum_scatter(grads, ("dp", "fsdp"), scatter_dimension=0, tiled=True).astype(F32)
    columns = grads.shape[1]
    items = nz * fs // 2
    dma = pltpu.SemaphoreType.DMA

    def blocks_of(n):
        return pltpu.VMEM((n, share, columns), BF16)

    return pl.pallas_call(
        reduce_kernel,
        in_specs=[ANY],
        out_specs=pl.BlockSpec(memory_space=pltpu.VMEM),
        out_shape=jax.ShapeDtypeStruct((share, columns), F32),
        scratch_shapes=[
            blocks_of(items), blocks_of(items), blocks_of(2 * nz), blocks_of(nz), blocks_of(nz), blocks_of(nz),
            dma, dma((items,)), dma((items,)), dma((2 * nz,)), dma((2 * nz,)), dma((nz,)), dma((nz,)),
            dma((nz,)), dma((nz,)), dma((nz,)), dma((nz,)),
        ],
        compiler_params=pltpu.CompilerParams(collective_id=1, has_side_effects=True, vmem_limit_bytes=VMEM_LIMIT),
        name="reduce",
    )(grads.reshape(items, 2, share, columns))


def local(
    inputs, cotangent, qkv_weight, proj_weight, expand_weight, contract_weight,
    prenorm, midnorm, lengths, dealing, holders, counts,
):
    micros, row_count, width = inputs.shape
    blocks = dealing.shape[1]
    rows = row_count // blocks
    hidden_units = contract_weight.shape[0]
    share = qkv_weight.shape[0]
    group = blocks * lax.axis_size("fsdp")
    slots = micros * blocks
    steps = slots // STEP_SLOTS
    total = slots * rows
    per = STEP_SLOTS * rows
    sds = jax.ShapeDtypeStruct
    tables = rope_tables(group, rows)
    table_specs = [whole(t.shape) for t in tables]
    lengths = lengths.reshape(micros, -1)
    holders = holders.reshape(micros * 2, blocks)
    x = inputs.reshape(total, width)
    cot = cotangent.reshape(total, width)

    gains = jnp.pad(jnp.stack([prenorm, midnorm], axis=1), ((0, 0), (0, PAIR - 2)))
    packed = jnp.concatenate([qkv_weight, expand_weight, contract_weight.T, proj_weight, gains], axis=1)
    w_all = gather(packed)
    columns = w_all.shape[1]
    gains = w_all[:, columns - PAIR : columns - PAIR + 2].astype(F32).T
    gain_pre, gain_mid = gains[0:1], gains[1:2]
    params = functools.partial(pltpu.CompilerParams, vmem_limit_bytes=VMEM_LIMIT, dimension_semantics=("arbitrary",))

    q, k, v, normed_one, to_next, to_prev = pl.pallas_call(
        functools.partial(qkv_kernel, blocks, group, rows, width),
        grid=(steps,),
        in_specs=[SMEM] * 3 + [by_step((per, width)), ANY, whole((1, width))] + table_specs,
        out_specs=[by_step((per, width))] * 4 + [whole((micros, rows, width)), whole((micros, rows + 16, width))],
        out_shape=[sds((total, width), BF16)] * 4
        + [sds((micros, rows, width), BF16), sds((micros, rows + 16, width), BF16)],
        scratch_shapes=[
            pltpu.VMEM((width, 3 * width), BF16),
            pltpu.VMEM((per, 3 * width), F32),
            pltpu.VMEM((per, PAIR), F32),
            pltpu.VMEM((per, PAIR), F32),
            pltpu.SemaphoreType.DMA,
        ],
        compiler_params=params(),
        name="qkv",
    )(lengths, dealing, counts, x, w_all, gain_pre, *tables)

    from_prev = shifted(to_next, "fsdp", 1)
    from_next = shifted(to_prev, "fsdp", -1)

    outs = pl.pallas_call(
        functools.partial(layer_kernel, blocks, group, rows, width, hidden_units),
        grid=(steps,),
        in_specs=[SMEM] * 4
        + [by_step((per, width)), whole((slots, rows, width)), whole((slots, rows, width))]
        + [whole((micros, rows, width)), whole((micros, rows + 16, width))]
        + [by_step((per, width))] * 2
        + [ANY, whole((1, width))]
        + table_specs,
        out_specs=[by_step((per, width))] * 3
        + [by_step((per, hidden_units)), by_step((per, width)), by_step((per, width))]
        + [by_step((per, 2 * hidden_units)), by_step((per, width)), by_step((per, width))]
        + [whole((slots, rows, width))] * 2
        + [whole((micros, rows, width))] * 2
        + [whole((8, width))],
        out_shape=[
            sds((total, width), BF16),
            sds((total, width), F32),
            sds((total, width), BF16),
            sds((total, hidden_units), BF16),
            sds((total, width), BF16),
            sds((total, width), BF16),
            sds((total, 2 * hidden_units), BF16),
            sds((total, width), BF16),
            sds((total, width), BF16),
            sds((slots, rows, width), F32),
            sds((slots, rows, width), F32),
            sds((micros, rows, width), BF16),
            sds((micros, rows, width), BF16),
            sds((8, width), F32),
        ],
        scratch_shapes=[
            pltpu.VMEM((width, width), BF16),
            pltpu.VMEM((width, 2 * hidden_units), BF16),
            pltpu.VMEM((width, hidden_units), BF16),
            pltpu.VMEM((STEP_SLOTS, 2 * rows, width), BF16),
            pltpu.VMEM((STEP_SLOTS, 2 * rows, width), BF16),
            pltpu.VMEM((STEP_SLOTS, 2 * rows, rows), F32),
            pltpu.VMEM((STEP_SLOTS, width // PAIR, 2 * rows, 2 * rows), F32),
            pltpu.VMEM((per, 2 * hidden_units), F32),
            pltpu.VMEM((per, width), F32),
            pltpu.VMEM((per, width), F32),
            pltpu.VMEM((per, width), F32),
            pltpu.VMEM((per, PAIR), F32),
            pltpu.VMEM((per, width), BF16),
            pltpu.VMEM((2, STEP_SLOTS, 2 * rows, width), F32),
            pltpu.SemaphoreType.DMA((3,)),
        ],
        compiler_params=params(),
        name="layer",
    )(
        lengths, dealing, holders, counts,
        q, k.reshape(slots, rows, width), v.reshape(slots, rows, width),
        from_prev, from_next, x, cot, w_all, gain_mid, *tables,
    )
    result, mid_grad, dq, hid, ffn_grad, normed_two, exp_grad, attended, attn_grad = outs[:9]
    dk, dv, back_prev, back_next, mid_term = outs[9:]

    ret_next = shifted(back_prev, "fsdp", -1)
    ret_prev = shifted(back_next, "fsdp", 1)
    term_expand = tn(normed_two, exp_grad).astype(BF16)
    term_contract = tn(ffn_grad, hid).astype(BF16)
    term_proj = tn(attended, attn_grad).astype(BF16)

    delta, input_grad, pre_term = pl.pallas_call(
        functools.partial(input_kernel, blocks, group, rows, width),
        grid=(steps,),
        in_specs=[SMEM] * 2
        + [by_step((per, width)), by_step((STEP_SLOTS, rows, width)), by_step((STEP_SLOTS, rows, width))]
        + [whole((micros, rows, width))] * 2
        + [by_step((per, width))] * 2
        + [ANY, whole((1, width))]
        + table_specs,
        out_specs=[by_step((per, 3 * width)), by_step((per, width)), whole((8, width))],
        out_shape=[sds((total, 3 * width), BF16), sds((total, width), BF16), sds((8, width), F32)],
        scratch_shapes=[
            pltpu.VMEM((width, 3 * width), BF16),
            pltpu.VMEM((per, width), F32),
            pltpu.SemaphoreType.DMA,
        ],
        compiler_params=params(),
        name="input",
    )(lengths, dealing, dq, dk, dv, ret_next, ret_prev, x, mid_grad, w_all, gain_pre, *tables)
    term_qkv = tn(normed_one, delta).astype(BF16)

    terms = jnp.stack([jnp.sum(pre_term, axis=0), jnp.sum(mid_term, axis=0)], axis=1)
    terms = jnp.pad(terms, ((0, 0), (0, PAIR - 2))).astype(BF16)
    grads = jnp.concatenate([term_qkv, term_expand, term_contract, term_proj, terms], axis=1)
    shard = reduce_scatter(grads, share)
    at = np.cumsum([0, 3 * width, 2 * hidden_units, hidden_units, width])
    return (
        result.reshape(inputs.shape),
        input_grad.reshape(inputs.shape),
        shard[:, at[0] : at[1]],
        shard[:, at[3] : at[4]],
        shard[:, at[1] : at[2]],
        shard[:, at[2] : at[3]].T,
        shard[:, at[4]],
        shard[:, at[4] + 1],
    )


def solution(mesh):
    both = ("dp", "fsdp")
    return jax.shard_map(
        local,
        mesh=mesh,
        in_specs=(
            P(None, both, None), P(None, both, None),
            P(both, None), P(both, None), P(both, None), P(None, both), P(both), P(both),
            P(None, "dp", None), P(None, both), P(None, None, both), P(None, both),
        ),
        out_specs=(
            P(None, both, None), P(None, both, None),
            P(both, None), P(both, None), P(both, None), P(None, both), P(both), P(both),
        ),
        check_vma=False,
    )
```

```python
import functools

import jax
import jax.numpy as jnp
import numpy as np
from jax import lax
from jax.experimental import pallas as pl
from jax.experimental.pallas import tpu as pltpu
from jax.sharding import PartitionSpec as P

HEAD_DIM = 64
PAIR = 128
STEP_SLOTS = 2
CHUNK = 32
norm_epsilon = 1e-05
rope_base = 10000.0
masked_score = -1e30
F32 = jnp.float32
BF16 = jnp.bfloat16
VMEM_LIMIT = 60 * 1024 * 1024


def nn(a, b):
    return lax.dot_general(a, b, (((1,), (0,)), ((), ())), preferred_element_type=F32)


def nt(a, b):
    return lax.dot_general(a, b, (((1,), (1,)), ((), ())), preferred_element_type=F32)


def tn(a, b):
    return lax.dot_general(a, b, (((0,), (0,)), ((), ())), preferred_element_type=F32)


def rope_tables(most_offset, block_rows):
    half = HEAD_DIM // 2
    freq = rope_base ** (-np.arange(half) * (2.0 / HEAD_DIM))
    freq = np.tile(freq, PAIR // half)
    sign = np.where(np.arange(PAIR) % HEAD_DIM < half, -1.0, 1.0)

    def pair(positions):
        angles = positions[:, None] * freq[None, :]
        return (
            jnp.asarray(np.cos(angles), F32),
            jnp.asarray(np.sin(angles) * sign[None, :], F32),
        )

    return (*pair(np.arange(most_offset) * float(block_rows)), *pair(np.arange(block_rows) * 1.0))


def slot_scalars(lengths, dealing, slot, blocks, group):
    micro = slot // blocks
    place = slot - micro * blocks
    block = dealing[micro, place]
    within = lax.rem(block, group)
    begin = jnp.int32(0)
    start = jnp.int32(0)
    ends = jnp.int32(0)
    for seq in range(lengths.shape[1]):
        begin = jnp.where(start <= within, start, begin)
        start = start + lengths[micro, seq]
        ends = ends + jnp.where(start - 1 == within, 1, 0)
    return micro, place, lax.rem(block, blocks), within - begin, ends > 0


def slot_angles(offset, ca, sa, cb, sb):
    first_c, first_s = ca[pl.ds(offset, 1), :], sa[pl.ds(offset, 1), :]
    return first_c * cb[...] - first_s * sb[...], first_s * cb[...] + first_c * sb[...]


def swap_halves(v):
    low = lax.broadcasted_iota(jnp.int32, v.shape, 1) % HEAD_DIM < HEAD_DIM // 2
    return jnp.where(low, pltpu.roll(v, PAIR - HEAD_DIM // 2, 1), pltpu.roll(v, HEAD_DIM // 2, 1))


def head_masks(dtype):
    low = lax.broadcasted_iota(jnp.int32, (1, PAIR), 1) < HEAD_DIM
    return low.astype(F32).astype(dtype), (1.0 - low.astype(F32)).astype(dtype)


def two_heads(tile):
    even, odd = head_masks(tile.dtype)
    half = tile.shape[0] // 2
    first, second = tile[:half], tile[half:]
    return jnp.concatenate([first * even, first * odd, second * even, second * odd], axis=0)


def from_heads(mixed):
    turned = mixed.T
    quarter = turned.shape[0] // 4
    even = lax.broadcasted_iota(jnp.int32, (quarter, PAIR), 1) < HEAD_DIM
    parts = [turned[n * quarter : (n + 1) * quarter] for n in range(4)]
    return jnp.concatenate([jnp.where(even, parts[0], parts[1]), jnp.where(even, parts[2], parts[3])], axis=0)


def chunk_rows(c, size=CHUNK):
    return pl.ds(pl.multiple_of(c * size, size), size)


def qkv_kernel(
    blocks, group, rows, width,
    lengths, dealing, counts, x, w_all, gain, ca, sa, cb, sb,
    q, k, v, normed, to_next, to_prev,
    w, full, cos, sin, sem,
):
    step = pl.program_id(0)
    half = rows // 2

    @pl.when(step == 0)
    def _():
        copy = pltpu.make_async_copy(w_all.at[:, pl.ds(0, 3 * width)], w, sem)
        copy.start()
        copy.wait()

    slots = [slot_scalars(lengths, dealing, step * STEP_SLOTS + t, blocks, group) for t in range(STEP_SLOTS)]
    for t, (_, _, _, offset, _) in enumerate(slots):
        c, s = slot_angles(offset, ca, sa, cb, sb)
        cos[t * rows : (t + 1) * rows, :] = c
        sin[t * rows : (t + 1) * rows, :] = s

    def norm(c, carry):
        at = chunk_rows(c)
        xf = x[at, :].astype(F32)
        centred = xf - jnp.mean(xf, axis=-1, keepdims=True)
        spread = jnp.mean(centred * centred, axis=-1, keepdims=True)
        normed[at, :] = (centred * lax.rsqrt(spread + norm_epsilon) * gain[...]).astype(BF16)
        return carry

    lax.fori_loop(0, STEP_SLOTS * rows // CHUNK, norm, 0)
    for n in range(0, 3 * width, 256):
        full[:, n : n + 256] = nn(normed[...], w[:, n : n + 256])

    def turn(c, carry):
        at = chunk_rows(c)
        co, si = cos[at, :], sin[at, :]
        for p in range(width // PAIR):
            lanes = slice(p * PAIR, (p + 1) * PAIR)
            for out, base in ((q, 0), (k, width)):
                tile = full[at, base + p * PAIR : base + (p + 1) * PAIR]
                out[at, lanes] = (tile * co + swap_halves(tile) * si).astype(BF16)
            v[at, lanes] = full[at, 2 * width + p * PAIR : 2 * width + (p + 1) * PAIR].astype(BF16)
        return carry

    lax.fori_loop(0, STEP_SLOTS * rows // CHUNK, turn, 0)
    for t, (micro, _, local, _, _) in enumerate(slots):
        base = t * rows

        @pl.when(local == blocks - 1)
        def _(micro=micro, base=base):
            to_next[micro, :half, :] = k[base + half : base + rows, :]
            to_next[micro, half:, :] = v[base + half : base + rows, :]

        @pl.when(local == 0)
        def _(micro=micro, base=base):
            to_prev[micro, :half, :] = k[base : base + half, :]
            to_prev[micro, half:rows, :] = v[base : base + half, :]
            valid = jnp.full((16, width), counts[micro, 0], jnp.int32).astype(F32)
            to_prev[micro, rows:, :] = valid.astype(BF16)


def layer_kernel(
    blocks, group, rows, width, hidden_units,
    lengths, dealing, holders, counts,
    q, k, v, from_prev, from_next, x, cot, w_all, gain, ca, sa, cb, sb,
    result, mid_grad, dq, hid, ffn_grad, normed, exp_grad, attended, attn_grad,
    dk, dv, back_prev, back_next, mid_term,
    wp, we, wc, kt, vt, bias, probs, prob_grad, low, expanded, wide, mid, hat, root, att_grad, tiles, sem,
):
    step = pl.program_id(0)
    half = rows // 2
    total = STEP_SLOTS * rows
    pairs = width // PAIR

    def weights():
        at = 3 * width
        out = []
        for place, (dst, cols) in enumerate(((we, 2 * hidden_units), (wc, hidden_units), (wp, width))):
            out.append(pltpu.make_async_copy(w_all.at[:, pl.ds(at, cols)], dst, sem.at[place]))
            at += cols
        return out

    @pl.when(step == 0)
    def _():
        for copy in weights():
            copy.start()
        dk[...] = jnp.zeros_like(dk)
        dv[...] = jnp.zeros_like(dv)
        mid_term[...] = jnp.zeros_like(mid_term)
        low[...] = jnp.zeros_like(low)

    slots = []
    for t in range(STEP_SLOTS):
        slot = step * STEP_SLOTS + t
        micro, place, local, offset, is_last = slot_scalars(lengths, dealing, slot, blocks, group)
        pred, succ = holders[micro * 2, place], holders[micro * 2 + 1, place]
        count = counts[micro, local]
        slots.append((slot, micro, pred, succ, offset, count))
        for src, dst, part in ((k, kt, 0), (v, vt, half)):
            @pl.when(pred < blocks)
            def _(src=src, dst=dst, t=t, micro=micro, pred=pred):
                dst[t, :half, :] = src[micro * blocks + pred, half:, :]

            @pl.when(pred >= blocks)
            def _(dst=dst, part=part, t=t, micro=micro):
                dst[t, :half, :] = from_prev[micro, part : part + half, :]

            dst[t, half : half + rows, :] = src[slot]

            @pl.when(succ < blocks)
            def _(src=src, dst=dst, t=t, micro=micro, succ=succ):
                dst[t, half + rows :, :] = src[micro * blocks + succ, :half, :]

            @pl.when(succ >= blocks)
            def _(dst=dst, part=part, t=t, micro=micro):
                dst[t, half + rows :, :] = from_next[micro, part : part + half, :]

        col = lax.broadcasted_iota(jnp.int32, (2 * rows, 2 * rows), 0)
        lane = lax.broadcasted_iota(jnp.int32, (2 * rows, 2 * rows), 1)
        row = lane // rows * half + lax.rem(lane, half)
        follow = counts[micro, lax.rem(local + 1, blocks)]
        remote = from_next[micro, rows : rows + 1, : 2 * rows].astype(F32)
        follow = jnp.where(succ < blocks, jnp.full((1, 2 * rows), follow, jnp.int32).astype(F32), remote)
        follow = half + rows + jnp.minimum(follow, half)
        ends = jnp.full((1, 2 * rows), half + count, jnp.int32).astype(F32)
        high = jnp.where(is_last, ends, follow)
        lowest = jnp.where(offset > 0, 0, half)
        allowed = (col >= row) & (col - row <= rows) & (col >= lowest) & (col.astype(F32) < high)
        bias[t] = jnp.where(allowed, 0.0, masked_score)

    scaled = jnp.asarray(HEAD_DIM**-0.5, BF16)
    places = [(t, p) for t in range(STEP_SLOTS) for p in range(pairs)]

    def lanes_of(p):
        return slice(p * PAIR, (p + 1) * PAIR)

    def queries(t, p):
        return two_heads(q[t * rows : (t + 1) * rows, lanes_of(p)] * scaled)

    for t, p in places:
        probs[t, p] = nt(kt[t, :, lanes_of(p)], queries(t, p))

    windows = [(slice(n * half, n * half + 3 * half), slice(n * PAIR, (n + 1) * PAIR)) for n in range(2)]

    def soften(p, carry):
        for t in range(STEP_SLOTS):
            for cols, lanes in windows:
                scores = probs[t, p, cols, lanes] + bias[t, cols, lanes]
                lifted = jnp.exp(scores - jnp.max(scores, axis=0, keepdims=True))
                prob = lifted * (1.0 / jnp.sum(lifted, axis=0, keepdims=True))
                probs[t, p, cols, lanes] = prob
                low[t, p, cols, lanes] = prob.astype(BF16)
        return carry

    lax.fori_loop(0, pairs, soften, 0)
    for t, p in places:
        mixed = tn(vt[t, :, lanes_of(p)], low[t, p])
        attended[t * rows : (t + 1) * rows, lanes_of(p)] = from_heads(mixed).astype(BF16)

    @pl.when(step == 0)
    def _():
        for copy in weights():
            copy.wait()

    def valid(c):
        per = rows // CHUNK
        inside = lax.rem(c, per) * CHUNK
        count = jnp.where(c < per, slots[0][5], slots[1][5])
        r = lax.broadcasted_iota(jnp.int32, (CHUNK, width), 0) + inside
        return r < count

    for n in range(0, width, 256):
        wide[:, n : n + 256] = nn(attended[...], wp[:, n : n + 256])

    def mid_norm(c, carry):
        at = chunk_rows(c)
        m = x[at, :].astype(F32) + jnp.where(valid(c), wide[at, :], 0.0)
        mid[at, :] = m
        centred = m - jnp.mean(m, axis=-1, keepdims=True)
        spread = jnp.mean(centred * centred, axis=-1, keepdims=True)
        scale = lax.rsqrt(spread + norm_epsilon)
        h = centred * scale
        hat[at, :] = h
        root[at, :] = jnp.broadcast_to(scale, (CHUNK, PAIR))
        normed[at, :] = (h * gain[...]).astype(BF16)
        ffn_grad[at, :] = jnp.where(valid(c), cot[at, :].astype(F32), 0.0).astype(BF16)
        return carry

    lax.fori_loop(0, total // CHUNK, mid_norm, 0)
    for n in range(0, 2 * hidden_units, 256):
        expanded[:, n : n + 256] = nn(normed[...], we[:, n : n + 256])

    def gate(c, carry):
        at = chunk_rows(c)
        for n in range(0, hidden_units, PAIR):
            a = expanded[at, n : n + PAIR]
            b = expanded[at, hidden_units + n : hidden_units + n + PAIR]
            phi = 0.5 + 0.5 * lax.erf(a * np.float32(0.5**0.5))
            density = np.float32((2 * np.pi) ** -0.5) * jnp.exp(a * a * -0.5)
            gelu = a * phi
            hid[at, n : n + PAIR] = (gelu * b).astype(BF16)
            expanded[at, n : n + PAIR] = b * (phi + a * density)
            expanded[at, hidden_units + n : hidden_units + n + PAIR] = gelu
        return carry

    lax.fori_loop(0, total // CHUNK, gate, 0)
    for n in range(0, width, 256):
        wide[:, n : n + 256] = nt(hid[...], wc[n : n + 256, :])

    def finish(c, carry):
        at = chunk_rows(c)
        result[at, :] = (mid[at, :] + jnp.where(valid(c), wide[at, :], 0.0)).astype(BF16)
        return carry

    lax.fori_loop(0, total // CHUNK, finish, 0)
    for n in range(0, hidden_units, 256):
        size = min(256, hidden_units - n)
        h = nn(ffn_grad[...], wc[:, n : n + size])
        exp_grad[:, n : n + size] = (h * expanded[:, n : n + size]).astype(BF16)
        exp_grad[:, hidden_units + n : hidden_units + n + size] = (
            h * expanded[:, hidden_units + n : hidden_units + n + size]
        ).astype(BF16)
    for n in range(0, width, 256):
        wide[:, n : n + 256] = nt(exp_grad[...], we[n : n + 256, :])

    def norm_back(c, carry):
        at = chunk_rows(c)
        g, h = wide[at, :], hat[at, :]
        gh = g * h
        mid_term[...] += jnp.sum(gh.reshape(CHUNK // 8, 8, width), axis=0)
        u = g * gain[...]
        mean_u = jnp.mean(u, axis=-1, keepdims=True)
        mean_uh = jnp.mean(u * h, axis=-1, keepdims=True)
        scale = jnp.concatenate([root[at, :]] * pairs, axis=1)
        m = cot[at, :].astype(F32) + (u - mean_u - h * mean_uh) * scale
        mid_grad[at, :] = m
        attn_grad[at, :] = jnp.where(valid(c), m, 0.0).astype(BF16)
        return carry

    lax.fori_loop(0, total // CHUNK, norm_back, 0)
    for n in range(0, width, 256):
        att_grad[:, n : n + 256] = nt(attn_grad[...], wp[n : n + 256, :]).astype(BF16)

    def grads(t, p):
        return two_heads(att_grad[t * rows : (t + 1) * rows, lanes_of(p)])

    for t, p in places:
        prob_grad[t, p] = nt(vt[t, :, lanes_of(p)], grads(t, p))
        tiles[1, t, :, lanes_of(p)] = nn(low[t, p], grads(t, p))

    def soften_back(p, carry):
        for t in range(STEP_SLOTS):
            for cols, lanes in windows:
                prob, grad = probs[t, p, cols, lanes], prob_grad[t, p, cols, lanes]
                mean = jnp.sum(prob * grad, axis=0, keepdims=True)
                low[t, p, cols, lanes] = (prob * (grad - mean)).astype(BF16)
        return carry

    lax.fori_loop(0, pairs, soften_back, 0)
    for t in range(STEP_SLOTS):
        c, s = slot_angles(slots[t][4], ca, sa, cb, sb)
        for p in range(pairs):
            tiles[0, t, :, lanes_of(p)] = nn(low[t, p], queries(t, p))
            g = from_heads(tn(kt[t, :, lanes_of(p)], low[t, p])) * np.float32(HEAD_DIM**-0.5)
            dq[t * rows : (t + 1) * rows, lanes_of(p)] = (g * c - swap_halves(g) * s).astype(BF16)
    for t, (slot, micro, pred, succ, _, _) in enumerate(slots):
        for which, out in ((0, dk), (1, dv)):
            part = which * half
            out[slot] += tiles[which, t, half : half + rows, :]

            @pl.when(pred < blocks)
            def _(out=out, which=which, t=t, micro=micro, pred=pred):
                out[micro * blocks + pred, half:, :] += tiles[which, t, :half, :]

            @pl.when(pred >= blocks)
            def _(part=part, which=which, t=t, micro=micro):
                back_prev[micro, part : part + half, :] = tiles[which, t, :half, :].astype(BF16)

            @pl.when(succ < blocks)
            def _(out=out, which=which, t=t, micro=micro, succ=succ):
                out[micro * blocks + succ, :half, :] += tiles[which, t, half + rows :, :]

            @pl.when(succ >= blocks)
            def _(part=part, which=which, t=t, micro=micro):
                back_next[micro, part : part + half, :] = tiles[which, t, half + rows :, :].astype(BF16)


def input_kernel(
    blocks, group, rows, width,
    lengths, dealing, dq, dk, dv, from_next, from_prev, x, mid_grad, w_all, gain, ca, sa, cb, sb,
    delta, input_grad, pre_term,
    w, wide, sem,
):
    step = pl.program_id(0)
    half = rows // 2

    @pl.when(step == 0)
    def _():
        copy = pltpu.make_async_copy(w_all.at[:, pl.ds(0, 3 * width)], w, sem)
        copy.start()
        copy.wait()
        pre_term[...] = jnp.zeros_like(pre_term)

    for t in range(STEP_SLOTS):
        micro, _, local, offset, _ = slot_scalars(lengths, dealing, step * STEP_SLOTS + t, blocks, group)
        c, s = slot_angles(offset, ca, sa, cb, sb)
        last = jnp.where(local == blocks - 1, 1.0, 0.0)
        first = jnp.where(local == 0, 1.0, 0.0)
        for top, weight, back in ((0, first, from_prev), (half, last, from_next)):
            at = slice(t * rows + top, t * rows + top + half)
            ct, st = c[top : top + half], s[top : top + half]
            for p in range(width // PAIR):
                lanes = slice(p * PAIR, (p + 1) * PAIR)
                g = dk[t, top : top + half, lanes] + weight * back[micro, :half, lanes].astype(F32)
                delta[at, lanes] = dq[at, lanes]
                delta[at, width + p * PAIR : width + (p + 1) * PAIR] = (g * ct - swap_halves(g) * st).astype(BF16)
                g = dv[t, top : top + half, lanes] + weight * back[micro, half:, lanes].astype(F32)
                delta[at, 2 * width + p * PAIR : 2 * width + (p + 1) * PAIR] = g.astype(BF16)
    for n in range(0, width, 256):
        wide[:, n : n + 256] = nt(delta[...], w[n : n + 256, :])

    def norm_back(c, carry):
        at = chunk_rows(c)
        xf = x[at, :].astype(F32)
        centred = xf - jnp.mean(xf, axis=-1, keepdims=True)
        spread = jnp.mean(centred * centred, axis=-1, keepdims=True)
        scale = lax.rsqrt(spread + norm_epsilon)
        h = centred * scale
        g = wide[at, :]
        pre_term[...] += jnp.sum((g * h).reshape(CHUNK // 8, 8, width), axis=0)
        u = g * gain[...]
        mean_u = jnp.mean(u, axis=-1, keepdims=True)
        mean_uh = jnp.mean(u * h, axis=-1, keepdims=True)
        input_grad[at, :] = (mid_grad[at, :] + (u - mean_u - h * mean_uh) * scale).astype(BF16)
        return carry

    lax.fori_loop(0, STEP_SLOTS * rows // CHUNK, norm_back, 0)


def shifted(block, axis, distance):
    devices = range(lax.axis_size(axis))
    route = [(i - distance, i) for i in devices if i - distance in devices]
    return lax.ppermute(block, axis, route)


def whole(shape):
    return pl.BlockSpec(shape, lambda i: (0,) * len(shape), pipeline_mode=pl.Buffered(1))


def by_step(shape):
    return pl.BlockSpec(shape, lambda i: (i,) + (0,) * (len(shape) - 1))


SMEM = pl.BlockSpec(memory_space=pltpu.SMEM)
ANY = pl.BlockSpec(memory_space=pl.ANY)


MESH = pl.DeviceIdType.MESH
LANES = 512


class Place:
    def __init__(self):
        self.nz, self.fs = lax.axis_size("dp"), lax.axis_size("fsdp")
        self.z = lax.axis_index("dp")
        self.f = lax.axis_index("fsdp")
        self.c = lax.rem(self.f, 2)
        first, second = self.f // 4, lax.rem(self.f // 2, 2)
        self.a2 = self.c * second + (1 - self.c) * first
        self.a3 = self.c * first + (1 - self.c) * second
        self.s2 = 4 - 2 * self.c
        self.s3 = 2 + 2 * self.c

    def square(self, x2, x3):
        return x2 * self.s2 + x3 * self.s3

    def at(self, z=None, x2=None, x3=None, other=False):
        z = self.z if z is None else z
        x2 = self.a2 if x2 is None else x2
        x3 = self.a3 if x3 is None else x3
        c = 1 - self.c if other else self.c
        return {"dp": z, "fsdp": self.square(x2, x3) + c}

    def greet(self):
        barrier = pltpu.get_barrier_semaphore()

        def signal(device):
            pl.semaphore_signal(barrier, inc=1, device_id=device, device_id_type=MESH)

        signal(self.at(x2=1 - self.a2))
        signal(self.at(x3=1 - self.a3))
        signal(self.at(other=True))
        for d in range(1, self.nz):
            signal(self.at(z=lax.rem(self.z + d, self.nz)))
        pl.semaphore_wait(barrier, 2 + self.nz)


def gather_kernel(parts, *refs):
    pieces, out, (own, send, recv, local_sem) = refs[:parts], refs[parts], refs[parts + 1 :]
    at = Place()
    z, nz, c, a2, a3 = at.z, at.nz, at.c, at.a2, at.a3
    begin = 0
    for piece in pieces:
        own[:, begin : begin + piece.shape[1]] = piece[...]
        begin += piece.shape[1]
    at.greet()
    started = []

    def item(zz, x2, x3, core):
        return zz * at.fs + at.square(x2, x3) + core

    def copy(src, it, slot, device):
        return pltpu.make_async_remote_copy(
            src_ref=src, dst_ref=out.at[it], send_sem=send.at[slot, it], recv_sem=recv.at[it],
            device_id=device, device_id_type=MESH,
        )

    def arrived(it):
        copy(out.at[it], it, 0, at.at(other=True)).wait_recv()

    def pass_on(src, it, targets):
        for slot, device in targets:
            copy(src, it, slot, device).start()
            started.append((it, slot, device))

    over = (0, at.at(other=True))
    over2 = (1, at.at(x2=1 - a2))
    over3 = (2, at.at(x3=1 - a3))
    order = line_order(z, nz)
    line = [(3 + d, at.at(z=zz)) for d, zz in enumerate(order)]
    mine = item(z, a2, a3, c)
    pass_on(own, mine, [over3, over2, *line, over])
    keep = pltpu.make_async_copy(own, out.at[mine], local_sem)
    keep.start()

    def forward(zz, x2, x3, targets):
        it = item(zz, x2, x3, c)
        arrived(it)
        pass_on(out.at[it], it, targets)

    def third(zz):
        for x2 in (a2, 1 - a2):
            forward(zz, x2, 1 - a3, [over])

    forward(z, 1 - a2, a3, [over3, over])
    for zz in order:
        forward(zz, a2, a3, [over3, over2, over])
    third(z)
    for zz in order:
        forward(zz, 1 - a2, a3, [over3, over])
    for zz in order:
        third(zz)

    def other(n, carry):
        arrived(2 * n + 1 - c)
        return carry

    lax.fori_loop(0, nz * at.fs // 2, other, 0)
    keep.wait()
    for it, slot, device in started:
        copy(out.at[it], it, slot, device).wait_send()


def line_order(z, nz):
    sign = 1 - 2 * (z // (nz // 2))
    return [lax.rem(z + sign * d + nz, nz) for d in range(1, nz)]


def gather(pieces):
    nz, fs = lax.axis_size("dp"), lax.axis_size("fsdp")
    rows, columns = pieces[0].shape[0], sum(piece.shape[1] for piece in pieces)
    if fs != 8 or rows % 8 or nz % 2:
        return lax.all_gather(jnp.concatenate(pieces, axis=1), ("dp", "fsdp"), axis=0, tiled=True)
    devices = nz * fs
    out = pl.pallas_call(
        functools.partial(gather_kernel, len(pieces)),
        in_specs=[pl.BlockSpec(memory_space=pltpu.VMEM)] * len(pieces),
        out_specs=ANY,
        out_shape=jax.ShapeDtypeStruct((devices, rows, columns), BF16),
        scratch_shapes=[
            pltpu.VMEM((rows, columns), BF16),
            pltpu.SemaphoreType.DMA((nz + 2, devices)),
            pltpu.SemaphoreType.DMA((devices,)),
            pltpu.SemaphoreType.DMA,
        ],
        compiler_params=pltpu.CompilerParams(collective_id=0, has_side_effects=True),
        name="gather",
    )(*pieces)
    return out.reshape(-1, columns)


def reduce_kernel(
    cuts, grads, *refs,
):
    outs, refs = refs[: len(cuts)], refs[len(cuts) :]
    own, side, over3, over2, line = refs[:5]
    own_sem, side_send, side_recv, send3, recv3, send2, recv2, send_z, recv_z = refs[5:]
    at = Place()
    z, nz, c, a2, a3 = at.z, at.nz, at.c, at.a2, at.a3
    columns = own.shape[2]
    squares = at.fs // 2
    at.greet()

    def remote(src, dst, send, recv, device):
        return pltpu.make_async_remote_copy(
            src_ref=src, dst_ref=dst, send_sem=send, recv_sem=recv, device_id=device, device_id_type=MESH
        )

    def item(zz, x2, x3):
        return zz * squares + at.square(x2, x3) // 2

    order = [*reversed(line_order(z, nz)), z]

    def partner_copy(i):
        return remote(grads.at[i, 1 - c], side.at[i], side_send.at[i], side_recv.at[i], at.at(other=True))

    for far in (1 - a2, a2):
        for zz in order:
            for x3 in (1 - a3, a3):
                partner_copy(item(zz, far, x3)).start()
    keep = pltpu.make_async_copy(grads.at[:, c], own, own_sem)
    keep.start()
    keep.wait()

    def add(i, *terms):
        for n in range(0, columns, LANES):
            lanes = slice(n, n + LANES)
            value = own[i, :, lanes].astype(F32)
            for ref, j in terms:
                value = value + ref[j, :, lanes].astype(F32)
            own[i, :, lanes] = value.astype(BF16)

    def copy3(i, slot):
        return remote(own.at[i], over3.at[slot], send3.at[slot], recv3.at[slot], at.at(x3=1 - a3))

    def copy2(i, k):
        return remote(own.at[i], over2.at[k], send2.at[k], recv2.at[k], at.at(x2=1 - a2))

    sent = []

    def send(one):
        one.start()
        sent.append(one)

    for k, zz in enumerate(order):
        for flag, x2 in ((1, 1 - a2), (0, a2)):
            i = item(zz, x2, 1 - a3)
            partner_copy(i).wait_recv()
            add(i, (side, i))
            send(copy3(i, 2 * k + flag))

    def third(k):
        i = item(order[k], a2, a3)
        copy2(i, k).wait_recv()
        add(i, (over2, k))
        if k < nz - 1:
            send(remote(own.at[i], line.at[z], send_z.at[k], recv_z.at[z], at.at(z=order[k])))

    for k, zz in enumerate(order):
        for flag, x2 in ((1, 1 - a2), (0, a2)):
            i = item(zz, x2, a3)
            partner_copy(i).wait_recv()
            copy3(i, 2 * k + flag).wait_recv()
            add(i, (side, i), (over3, 2 * k + flag))
            if flag:
                send(copy2(i, k))
        if k:
            third(k - 1)
    third(nz - 1)
    i = item(z, a2, a3)
    for zz in order[:-1]:
        remote(own.at[i], line.at[zz], send_z.at[0], recv_z.at[zz], at.at(z=zz)).wait_recv()
    for out, (begin, end) in zip(outs, cuts):
        for n in range(begin, end, PAIR):
            lanes = slice(n, n + PAIR)
            value = own[i, :, lanes].astype(F32)
            for zz in order[:-1]:
                value = value + line[zz, :, lanes].astype(F32)
            out[:, n - begin : n - begin + PAIR] = value
    for one in sent:
        one.wait_send()

    def partner_done(i, carry):
        partner_copy(i).wait_send()
        return carry

    lax.fori_loop(0, nz * squares, partner_done, 0)


def reduce_scatter(grads, share, cuts):
    nz, fs = lax.axis_size("dp"), lax.axis_size("fsdp")
    if fs != 8 or share % 8 or nz % 2:
        block = lax.psum_scatter(grads, ("dp", "fsdp"), scatter_dimension=0, tiled=True).astype(F32)
        return [block[:, begin:end] for begin, end in cuts]
    columns = grads.shape[1]
    items = nz * fs // 2
    dma = pltpu.SemaphoreType.DMA

    def blocks_of(n):
        return pltpu.VMEM((n, share, columns), BF16)

    return pl.pallas_call(
        functools.partial(reduce_kernel, cuts),
        in_specs=[ANY],
        out_specs=[pl.BlockSpec(memory_space=pltpu.VMEM)] * len(cuts),
        out_shape=[jax.ShapeDtypeStruct((share, end - begin), F32) for begin, end in cuts],
        scratch_shapes=[
            blocks_of(items), blocks_of(items), blocks_of(2 * nz), blocks_of(nz), blocks_of(nz),
            dma, dma((items,)), dma((items,)), dma((2 * nz,)), dma((2 * nz,)), dma((nz,)), dma((nz,)),
            dma((nz,)), dma((nz,)),
        ],
        compiler_params=pltpu.CompilerParams(collective_id=1, has_side_effects=True, vmem_limit_bytes=VMEM_LIMIT),
        name="reduce",
    )(grads.reshape(items, 2, share, columns))


def local(
    inputs, cotangent, qkv_weight, proj_weight, expand_weight, contract_weight,
    prenorm, midnorm, lengths, dealing, holders, counts,
):
    micros, row_count, width = inputs.shape
    blocks = dealing.shape[1]
    rows = row_count // blocks
    hidden_units = contract_weight.shape[0]
    share = qkv_weight.shape[0]
    group = blocks * lax.axis_size("fsdp")
    slots = micros * blocks
    steps = slots // STEP_SLOTS
    total = slots * rows
    per = STEP_SLOTS * rows
    sds = jax.ShapeDtypeStruct
    tables = rope_tables(group, rows)
    table_specs = [whole(t.shape) for t in tables]
    lengths = lengths.reshape(micros, -1)
    holders = holders.reshape(micros * 2, blocks)
    x = inputs.reshape(total, width)
    cot = cotangent.reshape(total, width)

    gains = jnp.pad(jnp.stack([prenorm, midnorm], axis=1), ((0, 0), (0, PAIR - 2)))
    w_all = gather([qkv_weight, expand_weight, contract_weight.T, proj_weight, gains])
    columns = w_all.shape[1]
    gains = w_all[:, columns - PAIR : columns - PAIR + 2].astype(F32).T
    gain_pre, gain_mid = gains[0:1], gains[1:2]
    params = functools.partial(pltpu.CompilerParams, vmem_limit_bytes=VMEM_LIMIT, dimension_semantics=("arbitrary",))

    q, k, v, normed_one, to_next, to_prev = pl.pallas_call(
        functools.partial(qkv_kernel, blocks, group, rows, width),
        grid=(steps,),
        in_specs=[SMEM] * 3 + [by_step((per, width)), ANY, whole((1, width))] + table_specs,
        out_specs=[by_step((per, width))] * 4 + [whole((micros, rows, width)), whole((micros, rows + 16, width))],
        out_shape=[sds((total, width), BF16)] * 4
        + [sds((micros, rows, width), BF16), sds((micros, rows + 16, width), BF16)],
        scratch_shapes=[
            pltpu.VMEM((width, 3 * width), BF16),
            pltpu.VMEM((per, 3 * width), F32),
            pltpu.VMEM((per, PAIR), F32),
            pltpu.VMEM((per, PAIR), F32),
            pltpu.SemaphoreType.DMA,
        ],
        compiler_params=params(),
        name="qkv",
    )(lengths, dealing, counts, x, w_all, gain_pre, *tables)

    from_prev = shifted(to_next, "fsdp", 1)
    from_next = shifted(to_prev, "fsdp", -1)

    outs = pl.pallas_call(
        functools.partial(layer_kernel, blocks, group, rows, width, hidden_units),
        grid=(steps,),
        in_specs=[SMEM] * 4
        + [by_step((per, width)), whole((slots, rows, width)), whole((slots, rows, width))]
        + [whole((micros, rows, width)), whole((micros, rows + 16, width))]
        + [by_step((per, width))] * 2
        + [ANY, whole((1, width))]
        + table_specs,
        out_specs=[by_step((per, width))] * 3
        + [by_step((per, hidden_units)), by_step((per, width)), by_step((per, width))]
        + [by_step((per, 2 * hidden_units)), by_step((per, width)), by_step((per, width))]
        + [whole((slots, rows, width))] * 2
        + [whole((micros, rows, width))] * 2
        + [whole((8, width))],
        out_shape=[
            sds((total, width), BF16),
            sds((total, width), F32),
            sds((total, width), BF16),
            sds((total, hidden_units), BF16),
            sds((total, width), BF16),
            sds((total, width), BF16),
            sds((total, 2 * hidden_units), BF16),
            sds((total, width), BF16),
            sds((total, width), BF16),
            sds((slots, rows, width), F32),
            sds((slots, rows, width), F32),
            sds((micros, rows, width), BF16),
            sds((micros, rows, width), BF16),
            sds((8, width), F32),
        ],
        scratch_shapes=[
            pltpu.VMEM((width, width), BF16),
            pltpu.VMEM((width, 2 * hidden_units), BF16),
            pltpu.VMEM((width, hidden_units), BF16),
            pltpu.VMEM((STEP_SLOTS, 2 * rows, width), BF16),
            pltpu.VMEM((STEP_SLOTS, 2 * rows, width), BF16),
            pltpu.VMEM((STEP_SLOTS, 2 * rows, 2 * rows), F32),
            pltpu.VMEM((STEP_SLOTS, width // PAIR, 2 * rows, 2 * rows), F32),
            pltpu.VMEM((STEP_SLOTS, width // PAIR, 2 * rows, 2 * rows), F32),
            pltpu.VMEM((STEP_SLOTS, width // PAIR, 2 * rows, 2 * rows), BF16),
            pltpu.VMEM((per, 2 * hidden_units), F32),
            pltpu.VMEM((per, width), F32),
            pltpu.VMEM((per, width), F32),
            pltpu.VMEM((per, width), F32),
            pltpu.VMEM((per, PAIR), F32),
            pltpu.VMEM((per, width), BF16),
            pltpu.VMEM((2, STEP_SLOTS, 2 * rows, width), F32),
            pltpu.SemaphoreType.DMA((3,)),
        ],
        compiler_params=params(),
        name="layer",
    )(
        lengths, dealing, holders, counts,
        q, k.reshape(slots, rows, width), v.reshape(slots, rows, width),
        from_prev, from_next, x, cot, w_all, gain_mid, *tables,
    )
    result, mid_grad, dq, hid, ffn_grad, normed_two, exp_grad, attended, attn_grad = outs[:9]
    dk, dv, back_prev, back_next, mid_term = outs[9:]

    ret_next = shifted(back_prev, "fsdp", -1)
    ret_prev = shifted(back_next, "fsdp", 1)
    term_expand = tn(normed_two, exp_grad).astype(BF16)
    term_contract = tn(ffn_grad, hid).astype(BF16)
    term_proj = tn(attended, attn_grad).astype(BF16)

    delta, input_grad, pre_term = pl.pallas_call(
        functools.partial(input_kernel, blocks, group, rows, width),
        grid=(steps,),
        in_specs=[SMEM] * 2
        + [by_step((per, width)), by_step((STEP_SLOTS, rows, width)), by_step((STEP_SLOTS, rows, width))]
        + [whole((micros, rows, width))] * 2
        + [by_step((per, width))] * 2
        + [ANY, whole((1, width))]
        + table_specs,
        out_specs=[by_step((per, 3 * width)), by_step((per, width)), whole((8, width))],
        out_shape=[sds((total, 3 * width), BF16), sds((total, width), BF16), sds((8, width), F32)],
        scratch_shapes=[
            pltpu.VMEM((width, 3 * width), BF16),
            pltpu.VMEM((per, width), F32),
            pltpu.SemaphoreType.DMA,
        ],
        compiler_params=params(),
        name="input",
    )(lengths, dealing, dq, dk, dv, ret_next, ret_prev, x, mid_grad, w_all, gain_pre, *tables)
    term_qkv = tn(normed_one, delta).astype(BF16)

    terms = jnp.stack([jnp.sum(pre_term, axis=0), jnp.sum(mid_term, axis=0)], axis=1)
    terms = jnp.pad(terms, ((0, 0), (0, PAIR - 2))).astype(BF16)
    grads = jnp.concatenate([term_qkv, term_expand, term_contract, term_proj, terms], axis=1)
    at = np.cumsum([0, 3 * width, 2 * hidden_units, hidden_units, width, PAIR]).tolist()
    qkv_sum, expand_sum, contract_sum, proj_sum, gain_sum = reduce_scatter(grads, share, list(zip(at, at[1:])))
    return (
        result.reshape(inputs.shape),
        input_grad.reshape(inputs.shape),
        qkv_sum,
        proj_sum,
        expand_sum,
        contract_sum.T,
        gain_sum[:, 0],
        gain_sum[:, 1],
    )


def solution(mesh):
    both = ("dp", "fsdp")
    return jax.shard_map(
        local,
        mesh=mesh,
        in_specs=(
            P(None, both, None), P(None, both, None),
            P(both, None), P(both, None), P(both, None), P(None, both), P(both), P(both),
            P(None, "dp", None), P(None, both), P(None, None, both), P(None, both),
        ),
        out_specs=(
            P(None, both, None), P(None, both, None),
            P(both, None), P(both, None), P(both, None), P(None, both), P(both), P(both),
        ),
        check_vma=False,
    )
```

```python
import functools

import jax
import jax.numpy as jnp
import numpy as np
from jax import lax
from jax.experimental import pallas as pl
from jax.experimental.pallas import tpu as pltpu
from jax.sharding import PartitionSpec as P

HEAD_DIM = 64
PAIR = 128
STEP_SLOTS = 2
CHUNK = 32
norm_epsilon = 1e-05
rope_base = 10000.0
masked_score = -1e30
F32 = jnp.float32
BF16 = jnp.bfloat16
VMEM_LIMIT = 60 * 1024 * 1024


def nn(a, b):
    return lax.dot_general(a, b, (((1,), (0,)), ((), ())), preferred_element_type=F32)


def nt(a, b):
    return lax.dot_general(a, b, (((1,), (1,)), ((), ())), preferred_element_type=F32)


def tn(a, b):
    return lax.dot_general(a, b, (((0,), (0,)), ((), ())), preferred_element_type=F32)


def rope_tables(most_offset, block_rows):
    half = HEAD_DIM // 2
    freq = rope_base ** (-np.arange(half) * (2.0 / HEAD_DIM))
    freq = np.tile(freq, PAIR // half)
    sign = np.where(np.arange(PAIR) % HEAD_DIM < half, -1.0, 1.0)

    def pair(positions):
        angles = positions[:, None] * freq[None, :]
        return (
            jnp.asarray(np.cos(angles), F32),
            jnp.asarray(np.sin(angles) * sign[None, :], F32),
        )

    return (*pair(np.arange(most_offset) * float(block_rows)), *pair(np.arange(block_rows) * 1.0))


def slot_scalars(lengths, dealing, slot, blocks, group):
    micro = slot // blocks
    place = slot - micro * blocks
    block = dealing[micro, place]
    within = lax.rem(block, group)
    begin = jnp.int32(0)
    start = jnp.int32(0)
    ends = jnp.int32(0)
    for seq in range(lengths.shape[1]):
        begin = jnp.where(start <= within, start, begin)
        start = start + lengths[micro, seq]
        ends = ends + jnp.where(start - 1 == within, 1, 0)
    return micro, place, lax.rem(block, blocks), within - begin, ends > 0


def slot_angles(offset, ca, sa, cb, sb):
    first_c, first_s = ca[pl.ds(offset, 1), :], sa[pl.ds(offset, 1), :]
    return first_c * cb[...] - first_s * sb[...], first_s * cb[...] + first_c * sb[...]


def swap_halves(v):
    low = lax.broadcasted_iota(jnp.int32, v.shape, 1) % HEAD_DIM < HEAD_DIM // 2
    return jnp.where(low, pltpu.roll(v, PAIR - HEAD_DIM // 2, 1), pltpu.roll(v, HEAD_DIM // 2, 1))


def head_masks(dtype):
    low = lax.broadcasted_iota(jnp.int32, (1, PAIR), 1) < HEAD_DIM
    return low.astype(F32).astype(dtype), (1.0 - low.astype(F32)).astype(dtype)


def two_heads(tile):
    even, odd = head_masks(tile.dtype)
    half = tile.shape[0] // 2
    first, second = tile[:half], tile[half:]
    return jnp.concatenate([first * even, first * odd, second * even, second * odd], axis=0)


def from_heads(mixed):
    turned = mixed.T
    quarter = turned.shape[0] // 4
    even = lax.broadcasted_iota(jnp.int32, (quarter, PAIR), 1) < HEAD_DIM
    parts = [turned[n * quarter : (n + 1) * quarter] for n in range(4)]
    return jnp.concatenate([jnp.where(even, parts[0], parts[1]), jnp.where(even, parts[2], parts[3])], axis=0)


def turned(out, ref):
    for n in range(0, ref.shape[1], PAIR):
        out[n : n + PAIR, :] = ref[:, n : n + PAIR].T


def chunk_rows(c, size=CHUNK):
    return pl.ds(pl.multiple_of(c * size, size), size)


def qkv_kernel(
    blocks, group, rows, width,
    lengths, dealing, counts, x, w_all, gain, ca, sa, cb, sb,
    q, k, v, normed_t, to_next, to_prev,
    w, full, cos, sin, normed, sem,
):
    step = pl.program_id(0)
    half = rows // 2

    @pl.when(step == 0)
    def _():
        copy = pltpu.make_async_copy(w_all.at[:, pl.ds(0, 3 * width)], w, sem)
        copy.start()
        copy.wait()

    slots = [slot_scalars(lengths, dealing, step * STEP_SLOTS + t, blocks, group) for t in range(STEP_SLOTS)]
    for t, (_, _, _, offset, _) in enumerate(slots):
        c, s = slot_angles(offset, ca, sa, cb, sb)
        cos[t * rows : (t + 1) * rows, :] = c
        sin[t * rows : (t + 1) * rows, :] = s

    def norm(c, carry):
        at = chunk_rows(c)
        xf = x[at, :].astype(F32)
        centred = xf - jnp.mean(xf, axis=-1, keepdims=True)
        spread = jnp.mean(centred * centred, axis=-1, keepdims=True)
        normed[at, :] = (centred * lax.rsqrt(spread + norm_epsilon) * gain[...]).astype(BF16)
        return carry

    lax.fori_loop(0, STEP_SLOTS * rows // CHUNK, norm, 0)
    turned(normed_t, normed)
    for n in range(0, 3 * width, 256):
        full[:, n : n + 256] = nn(normed[...], w[:, n : n + 256])

    def turn(c, carry):
        at = chunk_rows(c)
        co, si = cos[at, :], sin[at, :]
        for p in range(width // PAIR):
            lanes = slice(p * PAIR, (p + 1) * PAIR)
            for out, base in ((q, 0), (k, width)):
                tile = full[at, base + p * PAIR : base + (p + 1) * PAIR]
                out[at, lanes] = (tile * co + swap_halves(tile) * si).astype(BF16)
            v[at, lanes] = full[at, 2 * width + p * PAIR : 2 * width + (p + 1) * PAIR].astype(BF16)
        return carry

    lax.fori_loop(0, STEP_SLOTS * rows // CHUNK, turn, 0)
    for t, (micro, _, local, _, _) in enumerate(slots):
        base = t * rows

        @pl.when(local == blocks - 1)
        def _(micro=micro, base=base):
            to_next[micro, :half, :] = k[base + half : base + rows, :]
            to_next[micro, half:, :] = v[base + half : base + rows, :]

        @pl.when(local == 0)
        def _(micro=micro, base=base):
            to_prev[micro, :half, :] = k[base : base + half, :]
            to_prev[micro, half:rows, :] = v[base : base + half, :]
            valid = jnp.full((16, width), counts[micro, 0], jnp.int32).astype(F32)
            to_prev[micro, rows:, :] = valid.astype(BF16)


def layer_kernel(
    blocks, group, rows, width, hidden_units,
    lengths, dealing, holders, counts,
    q, k, v, from_prev, from_next, x, cot, w_all, gain, ca, sa, cb, sb,
    result, mid_grad, dq, hid, ffn_grad_t, normed_t, exp_grad, attended_t, attn_grad,
    dk, dv, back_prev, back_next, mid_term,
    ffn_grad, normed, attended, wp, we, wc, kt, vt, bias, probs, prob_grad, low, expanded, wide, mid, hat, root, att_grad, tiles, sem,
):
    step = pl.program_id(0)
    half = rows // 2
    total = STEP_SLOTS * rows
    pairs = width // PAIR

    def weights():
        at = 3 * width
        out = []
        for place, (dst, cols) in enumerate(((we, 2 * hidden_units), (wc, hidden_units), (wp, width))):
            out.append(pltpu.make_async_copy(w_all.at[:, pl.ds(at, cols)], dst, sem.at[place]))
            at += cols
        return out

    @pl.when(step == 0)
    def _():
        for copy in weights():
            copy.start()
        dk[...] = jnp.zeros_like(dk)
        dv[...] = jnp.zeros_like(dv)
        mid_term[...] = jnp.zeros_like(mid_term)
        low[...] = jnp.zeros_like(low)

    slots = []
    for t in range(STEP_SLOTS):
        slot = step * STEP_SLOTS + t
        micro, place, local, offset, is_last = slot_scalars(lengths, dealing, slot, blocks, group)
        pred, succ = holders[micro * 2, place], holders[micro * 2 + 1, place]
        count = counts[micro, local]
        slots.append((slot, micro, pred, succ, offset, count))
        for src, dst, part in ((k, kt, 0), (v, vt, half)):
            @pl.when(pred < blocks)
            def _(src=src, dst=dst, t=t, micro=micro, pred=pred):
                dst[t, :half, :] = src[micro * blocks + pred, half:, :]

            @pl.when(pred >= blocks)
            def _(dst=dst, part=part, t=t, micro=micro):
                dst[t, :half, :] = from_prev[micro, part : part + half, :]

            dst[t, half : half + rows, :] = src[slot]

            @pl.when(succ < blocks)
            def _(src=src, dst=dst, t=t, micro=micro, succ=succ):
                dst[t, half + rows :, :] = src[micro * blocks + succ, :half, :]

            @pl.when(succ >= blocks)
            def _(dst=dst, part=part, t=t, micro=micro):
                dst[t, half + rows :, :] = from_next[micro, part : part + half, :]

        col = lax.broadcasted_iota(jnp.int32, (2 * rows, 2 * rows), 0)
        lane = lax.broadcasted_iota(jnp.int32, (2 * rows, 2 * rows), 1)
        row = lane // rows * half + lax.rem(lane, half)
        follow = counts[micro, lax.rem(local + 1, blocks)]
        remote = from_next[micro, rows : rows + 1, : 2 * rows].astype(F32)
        follow = jnp.where(succ < blocks, jnp.full((1, 2 * rows), follow, jnp.int32).astype(F32), remote)
        follow = half + rows + jnp.minimum(follow, half)
        ends = jnp.full((1, 2 * rows), half + count, jnp.int32).astype(F32)
        high = jnp.where(is_last, ends, follow)
        lowest = jnp.where(offset > 0, 0, half)
        allowed = (col >= row) & (col - row <= rows) & (col >= lowest) & (col.astype(F32) < high)
        bias[t] = jnp.where(allowed, 0.0, masked_score)

    scaled = jnp.asarray(HEAD_DIM**-0.5, BF16)
    places = [(t, p) for t in range(STEP_SLOTS) for p in range(pairs)]

    def lanes_of(p):
        return slice(p * PAIR, (p + 1) * PAIR)

    def queries(t, p):
        return two_heads(q[t * rows : (t + 1) * rows, lanes_of(p)] * scaled)

    for t, p in places:
        probs[t, p] = nt(kt[t, :, lanes_of(p)], queries(t, p))

    windows = [(slice(n * half, n * half + 3 * half), slice(n * PAIR, (n + 1) * PAIR)) for n in range(2)]

    def soften(p, carry):
        for t in range(STEP_SLOTS):
            for cols, lanes in windows:
                scores = probs[t, p, cols, lanes] + bias[t, cols, lanes]
                lifted = jnp.exp(scores - jnp.max(scores, axis=0, keepdims=True))
                prob = lifted * (1.0 / jnp.sum(lifted, axis=0, keepdims=True))
                probs[t, p, cols, lanes] = prob
                low[t, p, cols, lanes] = prob.astype(BF16)
        return carry

    lax.fori_loop(0, pairs, soften, 0)
    for t, p in places:
        mixed = tn(vt[t, :, lanes_of(p)], low[t, p])
        attended[t * rows : (t + 1) * rows, lanes_of(p)] = from_heads(mixed).astype(BF16)

    @pl.when(step == 0)
    def _():
        for copy in weights():
            copy.wait()

    def valid(c):
        per = rows // CHUNK
        inside = lax.rem(c, per) * CHUNK
        count = jnp.where(c < per, slots[0][5], slots[1][5])
        r = lax.broadcasted_iota(jnp.int32, (CHUNK, width), 0) + inside
        return r < count

    for n in range(0, width, 256):
        wide[:, n : n + 256] = nn(attended[...], wp[:, n : n + 256])

    def mid_norm(c, carry):
        at = chunk_rows(c)
        m = x[at, :].astype(F32) + jnp.where(valid(c), wide[at, :], 0.0)
        mid[at, :] = m
        centred = m - jnp.mean(m, axis=-1, keepdims=True)
        spread = jnp.mean(centred * centred, axis=-1, keepdims=True)
        scale = lax.rsqrt(spread + norm_epsilon)
        h = centred * scale
        hat[at, :] = h
        root[at, :] = jnp.broadcast_to(scale, (CHUNK, PAIR))
        normed[at, :] = (h * gain[...]).astype(BF16)
        ffn_grad[at, :] = jnp.where(valid(c), cot[at, :].astype(F32), 0.0).astype(BF16)
        return carry

    lax.fori_loop(0, total // CHUNK, mid_norm, 0)
    turned(normed_t, normed)
    turned(ffn_grad_t, ffn_grad)
    turned(attended_t, attended)
    for n in range(0, 2 * hidden_units, 256):
        expanded[:, n : n + 256] = nn(normed[...], we[:, n : n + 256])

    def gate(c, carry):
        at = chunk_rows(c)
        for n in range(0, hidden_units, PAIR):
            a = expanded[at, n : n + PAIR]
            b = expanded[at, hidden_units + n : hidden_units + n + PAIR]
            phi = 0.5 + 0.5 * lax.erf(a * np.float32(0.5**0.5))
            density = np.float32((2 * np.pi) ** -0.5) * jnp.exp(a * a * -0.5)
            gelu = a * phi
            hid[at, n : n + PAIR] = (gelu * b).astype(BF16)
            expanded[at, n : n + PAIR] = b * (phi + a * density)
            expanded[at, hidden_units + n : hidden_units + n + PAIR] = gelu
        return carry

    lax.fori_loop(0, total // CHUNK, gate, 0)
    for n in range(0, width, 256):
        wide[:, n : n + 256] = nt(hid[...], wc[n : n + 256, :])

    def finish(c, carry):
        at = chunk_rows(c)
        result[at, :] = (mid[at, :] + jnp.where(valid(c), wide[at, :], 0.0)).astype(BF16)
        return carry

    lax.fori_loop(0, total // CHUNK, finish, 0)
    for n in range(0, hidden_units, 256):
        size = min(256, hidden_units - n)
        h = nn(ffn_grad[...], wc[:, n : n + size])
        exp_grad[:, n : n + size] = (h * expanded[:, n : n + size]).astype(BF16)
        exp_grad[:, hidden_units + n : hidden_units + n + size] = (
            h * expanded[:, hidden_units + n : hidden_units + n + size]
        ).astype(BF16)
    for n in range(0, width, 256):
        wide[:, n : n + 256] = nt(exp_grad[...], we[n : n + 256, :])

    def norm_back(c, carry):
        at = chunk_rows(c)
        g, h = wide[at, :], hat[at, :]
        gh = g * h
        mid_term[...] += jnp.sum(gh.reshape(CHUNK // 8, 8, width), axis=0)
        u = g * gain[...]
        mean_u = jnp.mean(u, axis=-1, keepdims=True)
        mean_uh = jnp.mean(u * h, axis=-1, keepdims=True)
        scale = jnp.concatenate([root[at, :]] * pairs, axis=1)
        m = cot[at, :].astype(F32) + (u - mean_u - h * mean_uh) * scale
        mid_grad[at, :] = m
        attn_grad[at, :] = jnp.where(valid(c), m, 0.0).astype(BF16)
        return carry

    lax.fori_loop(0, total // CHUNK, norm_back, 0)
    for n in range(0, width, 256):
        att_grad[:, n : n + 256] = nt(attn_grad[...], wp[n : n + 256, :]).astype(BF16)

    def grads(t, p):
        return two_heads(att_grad[t * rows : (t + 1) * rows, lanes_of(p)])

    for t, p in places:
        prob_grad[t, p] = nt(vt[t, :, lanes_of(p)], grads(t, p))
        tiles[1, t, :, lanes_of(p)] = nn(low[t, p], grads(t, p))

    def soften_back(p, carry):
        for t in range(STEP_SLOTS):
            for cols, lanes in windows:
                prob, grad = probs[t, p, cols, lanes], prob_grad[t, p, cols, lanes]
                mean = jnp.sum(prob * grad, axis=0, keepdims=True)
                low[t, p, cols, lanes] = (prob * (grad - mean)).astype(BF16)
        return carry

    lax.fori_loop(0, pairs, soften_back, 0)
    for t in range(STEP_SLOTS):
        c, s = slot_angles(slots[t][4], ca, sa, cb, sb)
        for p in range(pairs):
            tiles[0, t, :, lanes_of(p)] = nn(low[t, p], queries(t, p))
            g = from_heads(tn(kt[t, :, lanes_of(p)], low[t, p])) * np.float32(HEAD_DIM**-0.5)
            dq[t * rows : (t + 1) * rows, lanes_of(p)] = (g * c - swap_halves(g) * s).astype(BF16)
    for t, (slot, micro, pred, succ, _, _) in enumerate(slots):
        for which, out in ((0, dk), (1, dv)):
            part = which * half
            out[slot] += tiles[which, t, half : half + rows, :]

            @pl.when(pred < blocks)
            def _(out=out, which=which, t=t, micro=micro, pred=pred):
                out[micro * blocks + pred, half:, :] += tiles[which, t, :half, :]

            @pl.when(pred >= blocks)
            def _(part=part, which=which, t=t, micro=micro):
                back_prev[micro, part : part + half, :] = tiles[which, t, :half, :].astype(BF16)

            @pl.when(succ < blocks)
            def _(out=out, which=which, t=t, micro=micro, succ=succ):
                out[micro * blocks + succ, :half, :] += tiles[which, t, half + rows :, :]

            @pl.when(succ >= blocks)
            def _(part=part, which=which, t=t, micro=micro):
                back_next[micro, part : part + half, :] = tiles[which, t, half + rows :, :].astype(BF16)


def input_kernel(
    blocks, group, rows, width,
    lengths, dealing, dq, dk, dv, from_next, from_prev, x, mid_grad, w_all, gain, ca, sa, cb, sb,
    delta, input_grad, pre_term,
    w, wide, sem,
):
    step = pl.program_id(0)
    half = rows // 2

    @pl.when(step == 0)
    def _():
        copy = pltpu.make_async_copy(w_all.at[:, pl.ds(0, 3 * width)], w, sem)
        copy.start()
        copy.wait()
        pre_term[...] = jnp.zeros_like(pre_term)

    for t in range(STEP_SLOTS):
        micro, _, local, offset, _ = slot_scalars(lengths, dealing, step * STEP_SLOTS + t, blocks, group)
        c, s = slot_angles(offset, ca, sa, cb, sb)
        last = jnp.where(local == blocks - 1, 1.0, 0.0)
        first = jnp.where(local == 0, 1.0, 0.0)
        for top, weight, back in ((0, first, from_prev), (half, last, from_next)):
            at = slice(t * rows + top, t * rows + top + half)
            ct, st = c[top : top + half], s[top : top + half]
            for p in range(width // PAIR):
                lanes = slice(p * PAIR, (p + 1) * PAIR)
                g = dk[t, top : top + half, lanes] + weight * back[micro, :half, lanes].astype(F32)
                delta[at, lanes] = dq[at, lanes]
                delta[at, width + p * PAIR : width + (p + 1) * PAIR] = (g * ct - swap_halves(g) * st).astype(BF16)
                g = dv[t, top : top + half, lanes] + weight * back[micro, half:, lanes].astype(F32)
                delta[at, 2 * width + p * PAIR : 2 * width + (p + 1) * PAIR] = g.astype(BF16)
    for n in range(0, width, 256):
        wide[:, n : n + 256] = nt(delta[...], w[n : n + 256, :])

    def norm_back(c, carry):
        at = chunk_rows(c)
        xf = x[at, :].astype(F32)
        centred = xf - jnp.mean(xf, axis=-1, keepdims=True)
        spread = jnp.mean(centred * centred, axis=-1, keepdims=True)
        scale = lax.rsqrt(spread + norm_epsilon)
        h = centred * scale
        g = wide[at, :]
        pre_term[...] += jnp.sum((g * h).reshape(CHUNK // 8, 8, width), axis=0)
        u = g * gain[...]
        mean_u = jnp.mean(u, axis=-1, keepdims=True)
        mean_uh = jnp.mean(u * h, axis=-1, keepdims=True)
        input_grad[at, :] = (mid_grad[at, :] + (u - mean_u - h * mean_uh) * scale).astype(BF16)
        return carry

    lax.fori_loop(0, STEP_SLOTS * rows // CHUNK, norm_back, 0)


def shifted(block, axis, distance):
    devices = range(lax.axis_size(axis))
    route = [(i - distance, i) for i in devices if i - distance in devices]
    return lax.ppermute(block, axis, route)


def whole(shape):
    return pl.BlockSpec(shape, lambda i: (0,) * len(shape), pipeline_mode=pl.Buffered(1))


def by_step(shape):
    return pl.BlockSpec(shape, lambda i: (i,) + (0,) * (len(shape) - 1))


def by_column(shape):
    return pl.BlockSpec(shape, lambda i: (0, i))


SMEM = pl.BlockSpec(memory_space=pltpu.SMEM)
VMEM = pl.BlockSpec(memory_space=pltpu.VMEM)
ANY = pl.BlockSpec(memory_space=pl.ANY)


MESH = pl.DeviceIdType.MESH
LANES = 512


class Place:
    def __init__(self):
        self.nz, self.fs = lax.axis_size("dp"), lax.axis_size("fsdp")
        self.z = lax.axis_index("dp")
        self.f = lax.axis_index("fsdp")
        self.c = lax.rem(self.f, 2)
        first, second = self.f // 4, lax.rem(self.f // 2, 2)
        self.a2 = self.c * second + (1 - self.c) * first
        self.a3 = self.c * first + (1 - self.c) * second
        self.s2 = 4 - 2 * self.c
        self.s3 = 2 + 2 * self.c

    def square(self, x2, x3):
        return x2 * self.s2 + x3 * self.s3

    def at(self, z=None, x2=None, x3=None, other=False):
        z = self.z if z is None else z
        x2 = self.a2 if x2 is None else x2
        x3 = self.a3 if x3 is None else x3
        c = 1 - self.c if other else self.c
        return {"dp": z, "fsdp": self.square(x2, x3) + c}

    def greet(self, along=False):
        barrier = pltpu.get_barrier_semaphore()

        def signal(device):
            pl.semaphore_signal(barrier, inc=1, device_id=device, device_id_type=MESH)

        signal(self.at(x2=1 - self.a2))
        signal(self.at(x3=1 - self.a3))
        signal(self.at(other=True))
        for d in range(1, self.nz):
            signal(self.at(z=lax.rem(self.z + d, self.nz)))
        count = 2 + self.nz
        if along:
            last = self.fs - 1
            pl.when(self.f > 0)(lambda: signal({"dp": self.z, "fsdp": self.f - 1}))
            pl.when(self.f < last)(lambda: signal({"dp": self.z, "fsdp": self.f + 1}))
            count = count + (self.f + last) // self.fs + (2 * last - self.f) // self.fs
        pl.semaphore_wait(barrier, count)


def gather_kernel(parts, *refs):
    pieces, out, (own, send, recv, local_sem) = refs[:parts], refs[parts], refs[parts + 1 :]
    at = Place()
    z, nz, c, a2, a3 = at.z, at.nz, at.c, at.a2, at.a3
    begin = 0
    for piece in pieces:
        own[:, begin : begin + piece.shape[1]] = piece[...]
        begin += piece.shape[1]
    at.greet()
    started = []

    def item(zz, x2, x3, core):
        return zz * at.fs + at.square(x2, x3) + core

    def copy(src, it, slot, device):
        return pltpu.make_async_remote_copy(
            src_ref=src, dst_ref=out.at[it], send_sem=send.at[slot, it], recv_sem=recv.at[it],
            device_id=device, device_id_type=MESH,
        )

    def arrived(it):
        copy(out.at[it], it, 0, at.at(other=True)).wait_recv()

    def pass_on(src, it, targets):
        for slot, device in targets:
            copy(src, it, slot, device).start()
            started.append((it, slot, device))

    over = (0, at.at(other=True))
    over2 = (1, at.at(x2=1 - a2))
    over3 = (2, at.at(x3=1 - a3))
    order = line_order(z, nz)
    line = [(3 + d, at.at(z=zz)) for d, zz in enumerate(order)]
    mine = item(z, a2, a3, c)
    pass_on(own, mine, [over3, over2, *line, over])
    keep = pltpu.make_async_copy(own, out.at[mine], local_sem)
    keep.start()

    def forward(zz, x2, x3, targets):
        it = item(zz, x2, x3, c)
        arrived(it)
        pass_on(out.at[it], it, targets)

    def third(zz):
        for x2 in (a2, 1 - a2):
            forward(zz, x2, 1 - a3, [over])

    forward(z, 1 - a2, a3, [over3, over])
    for zz in order:
        forward(zz, a2, a3, [over3, over2, over])
    third(z)
    for zz in order:
        forward(zz, 1 - a2, a3, [over3, over])
    for zz in order:
        third(zz)

    def other(n, carry):
        arrived(2 * n + 1 - c)
        return carry

    lax.fori_loop(0, nz * at.fs // 2, other, 0)
    keep.wait()
    for it, slot, device in started:
        copy(out.at[it], it, slot, device).wait_send()


def line_order(z, nz):
    sign = 1 - 2 * (z // (nz // 2))
    return [lax.rem(z + sign * d + nz, nz) for d in range(1, nz)]


def gather(pieces):
    nz, fs = lax.axis_size("dp"), lax.axis_size("fsdp")
    rows, columns = pieces[0].shape[0], sum(piece.shape[1] for piece in pieces)
    if fs != 8 or rows % 8 or nz % 2:
        return lax.all_gather(jnp.concatenate(pieces, axis=1), ("dp", "fsdp"), axis=0, tiled=True)
    devices = nz * fs
    out = pl.pallas_call(
        functools.partial(gather_kernel, len(pieces)),
        in_specs=[pl.BlockSpec(memory_space=pltpu.VMEM)] * len(pieces),
        out_specs=ANY,
        out_shape=jax.ShapeDtypeStruct((devices, rows, columns), BF16),
        scratch_shapes=[
            pltpu.VMEM((rows, columns), BF16),
            pltpu.SemaphoreType.DMA((nz + 2, devices)),
            pltpu.SemaphoreType.DMA((devices,)),
            pltpu.SemaphoreType.DMA,
        ],
        compiler_params=pltpu.CompilerParams(collective_id=0, has_side_effects=True),
        name="gather",
    )(*pieces)
    return out.reshape(-1, columns)


def tail_kernel(
    cuts, blocks, group, rows,
    lengths, dealing, gain, ca, sa, cb, sb, mid_term, back_prev, back_next,
    dq, dk, dv, x, mid_grad, w_all, normed_one_t, normed_two_t, ffn_grad_t, attended_t, exp_grad, hid, attn_grad,
    input_grad, *refs,
):
    outs, refs = refs[: len(cuts)], refs[len(cuts) :]
    grads, side, over3, over2, line, from_next, from_prev = refs[:7]
    n2, fg, att, eg, hd, ag, w, n1, wide, pre_term, dqs, dks, dvs, xs, mids, done = refs[7:23]
    load_sem, step_sem, done_sem, halo_send, halo_recv = refs[23:28]
    side_send, side_recv, send3, recv3, send2, recv2, send_z, recv_z = refs[28:]
    at = Place()
    z, nz, c, a2, a3, f, fs = at.z, at.nz, at.c, at.a2, at.a3, at.f, at.fs
    share = grads.shape[2]
    width = x.shape[1]
    half = rows // 2
    per = STEP_SLOTS * rows
    steps = x.shape[0] // per
    at.greet(along=True)

    loads = [(normed_two_t, n2), (exp_grad, eg), (ffn_grad_t, fg), (hid, hd), (attended_t, att), (attn_grad, ag)]
    loads += [(w_all.at[:, pl.ds(0, 3 * width)], w), (normed_one_t, n1)]
    loads = [pltpu.make_async_copy(src, dst, load_sem.at[n]) for n, (src, dst) in enumerate(loads)]

    def remote(src, dst, send, recv, device):
        return pltpu.make_async_remote_copy(
            src_ref=src, dst_ref=dst, send_sem=send, recv_sem=recv, device_id=device, device_id_type=MESH
        )

    loads[0].start()
    loads[1].start()
    halo_down = remote(back_prev, from_next, halo_send.at[0], halo_recv.at[0], {"dp": z, "fsdp": f - 1})
    halo_up = remote(back_next, from_prev, halo_send.at[1], halo_recv.at[1], {"dp": z, "fsdp": f + 1})
    pl.when(f > 0)(halo_down.start)
    pl.when(f < fs - 1)(halo_up.start)
    for one in loads[2:]:
        one.start()

    def step_loads(i):
        n = i % 2
        srcs = [
            (dq.at[pl.ds(i * per, per)], dqs), (dk.at[pl.ds(i * STEP_SLOTS, STEP_SLOTS)], dks),
            (dv.at[pl.ds(i * STEP_SLOTS, STEP_SLOTS)], dvs), (x.at[pl.ds(i * per, per)], xs),
            (mid_grad.at[pl.ds(i * per, per)], mids),
        ]
        return [pltpu.make_async_copy(src, dst.at[n], step_sem.at[n, m]) for m, (src, dst) in enumerate(srcs)]

    for one in step_loads(0):
        one.start()
    order = [*reversed(line_order(z, nz)), z]
    sent = []

    def send(one):
        one.start()
        sent.append(one)

    class Part:
        def __init__(self, n, begin, end):
            self.n, self.cols, self.begin, self.end = n, slice(begin, end), begin, end

        def mine(self, zz, x2, x3):
            return grads.at[zz, at.square(x2, x3) + c, :, self.cols]

        def partner(self, zz, x2, x3):
            sq = at.square(x2, x3)
            i = zz * (fs // 2) + sq // 2
            return remote(
                grads.at[zz, sq + 1 - c, :, self.cols], side.at[i, :, self.cols],
                side_send.at[self.n, i], side_recv.at[self.n, i], at.at(other=True),
            )

        def copy3(self, k, flag):
            x2 = 1 - a2 if flag else a2
            j = 2 * k + flag
            return remote(
                self.mine(order[k], x2, 1 - a3), over3.at[j, :, self.cols],
                send3.at[self.n, j], recv3.at[self.n, j], at.at(x3=1 - a3),
            )

        def copy2(self, k):
            return remote(
                self.mine(order[k], 1 - a2, a3), over2.at[k, :, self.cols],
                send2.at[self.n, k], recv2.at[self.n, k], at.at(x2=1 - a2),
            )

        def copy_z(self, k, source, target):
            return remote(
                self.mine(target, a2, a3), line.at[source, :, self.cols],
                send_z.at[self.n, k], recv_z.at[self.n, source], at.at(z=target),
            )

        def add(self, zz, x2, x3, *terms):
            mine = at.square(x2, x3) + c
            for n in range(self.begin, self.end, LANES):
                lanes = slice(n, min(n + LANES, self.end))
                value = grads[zz, mine, :, lanes].astype(F32)
                for ref, j in terms:
                    value = value + ref[j, :, lanes].astype(F32)
                grads[zz, mine, :, lanes] = value.astype(BF16)

        def side_of(self, zz, x2, x3):
            return side, zz * (fs // 2) + at.square(x2, x3) // 2

        def put(self, k):
            for far in (1 - a2, a2):
                for x3 in (1 - a3, a3):
                    send(self.partner(order[k], far, x3))

        def first(self, k):
            zz = order[k]
            for flag, x2 in ((1, 1 - a2), (0, a2)):
                self.partner(zz, x2, 1 - a3).wait_recv()
                self.add(zz, x2, 1 - a3, self.side_of(zz, x2, 1 - a3))
                send(self.copy3(k, flag))

        def second(self, k):
            zz = order[k]
            for flag, x2 in ((1, 1 - a2), (0, a2)):
                self.partner(zz, x2, a3).wait_recv()
                self.copy3(k, flag).wait_recv()
                self.add(zz, x2, a3, self.side_of(zz, x2, a3), (over3, 2 * k + flag))
                if flag:
                    send(self.copy2(k))

        def third(self, k):
            self.copy2(k).wait_recv()
            self.add(order[k], a2, a3, (over2, k))
            if k < nz - 1:
                send(self.copy_z(k, z, order[k]))

        def finish(self):
            for zz in order[:-1]:
                self.copy_z(0, zz, z).wait_recv()
            mine = at.square(a2, a3) + c
            for out, (begin, end) in zip(outs, cuts):
                if begin < self.begin or end > self.end:
                    continue
                for n in range(begin, end, PAIR):
                    lanes = slice(n, n + PAIR)
                    value = grads[z, mine, :, lanes].astype(F32)
                    for zz in order[:-1]:
                        value = value + line[zz, :, lanes].astype(F32)
                    out[:, n - begin : n - begin + PAIR] = value

    def product(k, lhs, rhs, begin):
        block = lhs[pl.ds(pl.multiple_of(order[k] * (fs * share), 16), fs * share), :]
        columns = rhs.shape[1]
        for n in range(0, columns, 256):
            size = min(256, columns - n)
            value = nn(block, rhs[:, n : n + size]).astype(BF16)
            grads[order[k], :, :, begin + n : begin + n + size] = value.reshape(fs, share, size)

    early = Part(0, cuts[0][0], cuts[2][1])
    late = Part(1, cuts[3][0], cuts[4][1])

    def early_block(k):
        for n, (lhs, rhs) in enumerate(((n2, eg), (fg, hd), (att, ag))):
            if k == 0:
                loads[2 * n].wait()
                loads[2 * n + 1].wait()
            product(k, lhs, rhs, cuts[n][0])
        early.put(k)

    delta = eg

    def write_back(i):
        return pltpu.make_async_copy(done.at[i % 2], input_grad.at[pl.ds(i * per, per)], done_sem.at[i % 2])

    def input_step(i):
        n = i % 2
        for one in step_loads(i):
            one.wait()
        if i + 1 < steps:
            for one in step_loads(i + 1):
                one.start()
        base = i * per
        for t in range(STEP_SLOTS):
            micro, _, local, offset, _ = slot_scalars(lengths, dealing, i * STEP_SLOTS + t, blocks, group)
            micro = (i * STEP_SLOTS + t) // blocks
            co, si = slot_angles(offset, ca, sa, cb, sb)
            last = jnp.where(local == blocks - 1, 1.0, 0.0)
            head = jnp.where(local == 0, 1.0, 0.0)
            for top, weight, back in ((0, head, from_prev), (half, last, from_next)):
                rows_in = slice(t * rows + top, t * rows + top + half)
                rows_out = slice(base + t * rows + top, base + t * rows + top + half)
                ct, st = co[top : top + half], si[top : top + half]
                for p in range(width // PAIR):
                    lanes = slice(p * PAIR, (p + 1) * PAIR)
                    g = dks[n, t, top : top + half, lanes] + weight * back[micro, :half, lanes].astype(F32)
                    delta[rows_out, lanes] = dqs[n, rows_in, lanes]
                    delta[rows_out, width + p * PAIR : width + (p + 1) * PAIR] = (
                        g * ct - swap_halves(g) * st
                    ).astype(BF16)
                    g = dvs[n, t, top : top + half, lanes] + weight * back[micro, half:, lanes].astype(F32)
                    delta[rows_out, 2 * width + p * PAIR : 2 * width + (p + 1) * PAIR] = g.astype(BF16)
        for m in range(0, width, 256):
            wide[:, m : m + 256] = nt(delta[base : base + per, :], w[m : m + 256, :])
        if i >= 2:
            write_back(i - 2).wait()

        def norm_back(j, carry):
            rows_at = chunk_rows(j)
            xf = xs[n, rows_at, :].astype(F32)
            centred = xf - jnp.mean(xf, axis=-1, keepdims=True)
            spread = jnp.mean(centred * centred, axis=-1, keepdims=True)
            scale = lax.rsqrt(spread + norm_epsilon)
            h = centred * scale
            g = wide[rows_at, :]
            pre_term[...] += jnp.sum((g * h).reshape(CHUNK // 8, 8, width), axis=0)
            u = g * gain[...]
            mean_u = jnp.mean(u, axis=-1, keepdims=True)
            mean_uh = jnp.mean(u * h, axis=-1, keepdims=True)
            done[n, rows_at, :] = (mids[n, rows_at, :] + (u - mean_u - h * mean_uh) * scale).astype(BF16)
            return carry

        lax.fori_loop(0, per // CHUNK, norm_back, 0)
        write_back(i).start()

    pre_term[...] = jnp.zeros_like(pre_term)

    @pl.when(f == fs - 1)
    def _():
        from_next[...] = jnp.zeros_like(from_next)

    @pl.when(f == 0)
    def _():
        from_prev[...] = jnp.zeros_like(from_prev)

    def halos():
        pl.when(f < fs - 1)(halo_down.wait_recv)
        pl.when(f > 0)(halo_up.wait_recv)
        loads[6].wait()

    work = [functools.partial(early_block, k) for k in range(nz)]
    work += [halos, *[functools.partial(input_step, i) for i in range(steps)]]
    stages = [[] for _ in work]
    for k in range(nz):
        stages[k + 1].append(functools.partial(early.first, k))
        for lag, stage in ((2, early.second), (3, early.third)):
            stages[k + lag].append(functools.partial(stage, k))
    stages[min(nz + 3, len(work) - 1)].append(early.finish)
    for one, then in zip(work, stages):
        one()
        for stage in then:
            stage()

    loads[7].wait()
    row = lax.broadcasted_iota(jnp.int32, (PAIR, width), 0)
    pre_sum = jnp.sum(pre_term[...], axis=0, keepdims=True)
    mid_sum = jnp.sum(mid_term[...], axis=0, keepdims=True)
    terms = jnp.where(row == 0, pre_sum, jnp.where(row == 1, mid_sum, 0.0))
    grads[:, :, :, cuts[4][0] : cuts[4][1]] = terms.T.astype(BF16).reshape(nz, fs, share, PAIR)
    for k in range(nz):
        product(k, n1, delta, cuts[3][0])
        late.put(k)
        if k:
            late.first(k - 1)
    late.first(nz - 1)
    for k in range(nz):
        late.second(k)
        if k:
            late.third(k - 1)
    late.third(nz - 1)
    late.finish()
    for one in sent:
        one.wait_send()
    pl.when(f > 0)(halo_down.wait_send)
    pl.when(f < fs - 1)(halo_up.wait_send)
    for i in range(max(steps - 2, 0), steps):
        write_back(i).wait()


def tail(
    cuts, blocks, group, rows, share, lengths, dealing, gain, tables, mid_term, back_prev, back_next,
    dq, dk, dv, x, mid_grad, w_all, *operands,
):
    nz, fs = lax.axis_size("dp"), lax.axis_size("fsdp")
    total, width = x.shape
    per = STEP_SLOTS * rows
    columns = cuts[-1][1]
    items = nz * fs // 2
    dma = pltpu.SemaphoreType.DMA

    def blocks_of(n):
        return pltpu.VMEM((n, share, columns), BF16)

    def like(a):
        return pltpu.VMEM(a.shape, a.dtype)

    n1, n2, fg, att, eg, hid, ag = operands
    return pl.pallas_call(
        functools.partial(tail_kernel, cuts, blocks, group, rows),
        in_specs=[SMEM] * 2 + [VMEM] * 6 + [ANY] * (8 + len(operands)),
        out_specs=[ANY] + [VMEM] * len(cuts),
        out_shape=[jax.ShapeDtypeStruct((total, width), BF16)]
        + [jax.ShapeDtypeStruct((share, end - begin), F32) for begin, end in cuts],
        scratch_shapes=[
            pltpu.VMEM((nz, fs, share, columns), BF16),
            blocks_of(items), blocks_of(2 * nz), blocks_of(nz), blocks_of(nz), like(back_prev), like(back_prev),
            like(n2), like(fg), like(att), like(eg), like(hid), like(ag),
            pltpu.VMEM((width, 3 * width), BF16), like(n1), pltpu.VMEM((per, width), F32), pltpu.VMEM((8, width), F32),
            pltpu.VMEM((2, per, width), BF16), pltpu.VMEM((2, STEP_SLOTS, rows, width), F32),
            pltpu.VMEM((2, STEP_SLOTS, rows, width), F32), pltpu.VMEM((2, per, width), BF16),
            pltpu.VMEM((2, per, width), F32), pltpu.VMEM((2, per, width), BF16),
            dma((8,)), dma((2, 5)), dma((2,)), dma((2,)), dma((2,)),
            dma((2, items)), dma((2, items)), dma((2, 2 * nz)), dma((2, 2 * nz)), dma((2, nz)), dma((2, nz)),
            dma((2, nz)), dma((2, nz)),
        ],
        compiler_params=pltpu.CompilerParams(collective_id=1, has_side_effects=True, vmem_limit_bytes=VMEM_LIMIT),
        name="tail",
    )(lengths, dealing, gain, *tables, mid_term, back_prev, back_next, dq, dk, dv, x, mid_grad, w_all, *operands)


def local(
    inputs, cotangent, qkv_weight, proj_weight, expand_weight, contract_weight,
    prenorm, midnorm, lengths, dealing, holders, counts,
):
    micros, row_count, width = inputs.shape
    blocks = dealing.shape[1]
    rows = row_count // blocks
    hidden_units = contract_weight.shape[0]
    share = qkv_weight.shape[0]
    group = blocks * lax.axis_size("fsdp")
    slots = micros * blocks
    steps = slots // STEP_SLOTS
    total = slots * rows
    per = STEP_SLOTS * rows
    sds = jax.ShapeDtypeStruct
    tables = rope_tables(group, rows)
    table_specs = [whole(t.shape) for t in tables]
    lengths = lengths.reshape(micros, -1)
    holders = holders.reshape(micros * 2, blocks)
    x = inputs.reshape(total, width)
    cot = cotangent.reshape(total, width)

    gains = jnp.pad(jnp.stack([prenorm, midnorm], axis=1), ((0, 0), (0, PAIR - 2)))
    w_all = gather([qkv_weight, expand_weight, contract_weight.T, proj_weight, gains])
    columns = w_all.shape[1]
    gains = w_all[:, columns - PAIR : columns - PAIR + 2].astype(F32).T
    gain_pre, gain_mid = gains[0:1], gains[1:2]
    params = functools.partial(pltpu.CompilerParams, vmem_limit_bytes=VMEM_LIMIT, dimension_semantics=("arbitrary",))

    q, k, v, normed_one_t, to_next, to_prev = pl.pallas_call(
        functools.partial(qkv_kernel, blocks, group, rows, width),
        grid=(steps,),
        in_specs=[SMEM] * 3 + [by_step((per, width)), ANY, whole((1, width))] + table_specs,
        out_specs=[by_step((per, width))] * 3
        + [by_column((width, per)), whole((micros, rows, width)), whole((micros, rows + 16, width))],
        out_shape=[sds((total, width), BF16)] * 3
        + [sds((width, total), BF16)]
        + [sds((micros, rows, width), BF16), sds((micros, rows + 16, width), BF16)],
        scratch_shapes=[
            pltpu.VMEM((width, 3 * width), BF16),
            pltpu.VMEM((per, 3 * width), F32),
            pltpu.VMEM((per, PAIR), F32),
            pltpu.VMEM((per, PAIR), F32),
            pltpu.VMEM((per, width), BF16),
            pltpu.SemaphoreType.DMA,
        ],
        compiler_params=params(),
        name="qkv",
    )(lengths, dealing, counts, x, w_all, gain_pre, *tables)

    from_prev = shifted(to_next, "fsdp", 1)
    from_next = shifted(to_prev, "fsdp", -1)

    outs = pl.pallas_call(
        functools.partial(layer_kernel, blocks, group, rows, width, hidden_units),
        grid=(steps,),
        in_specs=[SMEM] * 4
        + [by_step((per, width)), whole((slots, rows, width)), whole((slots, rows, width))]
        + [whole((micros, rows, width)), whole((micros, rows + 16, width))]
        + [by_step((per, width))] * 2
        + [ANY, whole((1, width))]
        + table_specs,
        out_specs=[by_step((per, width))] * 3
        + [by_step((per, hidden_units)), by_column((width, per)), by_column((width, per))]
        + [by_step((per, 2 * hidden_units)), by_column((width, per)), by_step((per, width))]
        + [whole((slots, rows, width))] * 2
        + [whole((micros, rows, width))] * 2
        + [whole((8, width))],
        out_shape=[
            sds((total, width), BF16),
            sds((total, width), F32),
            sds((total, width), BF16),
            sds((total, hidden_units), BF16),
            sds((width, total), BF16),
            sds((width, total), BF16),
            sds((total, 2 * hidden_units), BF16),
            sds((width, total), BF16),
            sds((total, width), BF16),
            sds((slots, rows, width), F32),
            sds((slots, rows, width), F32),
            sds((micros, rows, width), BF16),
            sds((micros, rows, width), BF16),
            sds((8, width), F32),
        ],
        scratch_shapes=[
            pltpu.VMEM((per, width), BF16),
            pltpu.VMEM((per, width), BF16),
            pltpu.VMEM((per, width), BF16),
            pltpu.VMEM((width, width), BF16),
            pltpu.VMEM((width, 2 * hidden_units), BF16),
            pltpu.VMEM((width, hidden_units), BF16),
            pltpu.VMEM((STEP_SLOTS, 2 * rows, width), BF16),
            pltpu.VMEM((STEP_SLOTS, 2 * rows, width), BF16),
            pltpu.VMEM((STEP_SLOTS, 2 * rows, 2 * rows), F32),
            pltpu.VMEM((STEP_SLOTS, width // PAIR, 2 * rows, 2 * rows), F32),
            pltpu.VMEM((STEP_SLOTS, width // PAIR, 2 * rows, 2 * rows), F32),
            pltpu.VMEM((STEP_SLOTS, width // PAIR, 2 * rows, 2 * rows), BF16),
            pltpu.VMEM((per, 2 * hidden_units), F32),
            pltpu.VMEM((per, width), F32),
            pltpu.VMEM((per, width), F32),
            pltpu.VMEM((per, width), F32),
            pltpu.VMEM((per, PAIR), F32),
            pltpu.VMEM((per, width), BF16),
            pltpu.VMEM((2, STEP_SLOTS, 2 * rows, width), F32),
            pltpu.SemaphoreType.DMA((3,)),
        ],
        compiler_params=params(),
        name="layer",
    )(
        lengths, dealing, holders, counts,
        q, k.reshape(slots, rows, width), v.reshape(slots, rows, width),
        from_prev, from_next, x, cot, w_all, gain_mid, *tables,
    )
    result, mid_grad, dq, hid, ffn_grad_t, normed_two_t, exp_grad, attended_t, attn_grad = outs[:9]
    dk, dv, back_prev, back_next, mid_term = outs[9:]

    at = np.cumsum([0, 2 * hidden_units, hidden_units, width, 3 * width, PAIR]).tolist()
    cuts = list(zip(at, at[1:]))
    nz, fs = lax.axis_size("dp"), lax.axis_size("fsdp")
    if fs == 8 and share % 8 == 0 and nz % 2 == 0:
        input_grad, expand_sum, contract_sum, proj_sum, qkv_sum, gain_sum = tail(
            cuts, blocks, group, rows, share, lengths, dealing, gain_pre, tables, mid_term, back_prev, back_next,
            dq, dk, dv, x, mid_grad, w_all,
            normed_one_t, normed_two_t, ffn_grad_t, attended_t, exp_grad, hid, attn_grad,
        )
    else:
        ret_next = shifted(back_prev, "fsdp", -1)
        ret_prev = shifted(back_next, "fsdp", 1)
        delta, input_grad, pre_term = pl.pallas_call(
            functools.partial(input_kernel, blocks, group, rows, width),
            grid=(steps,),
            in_specs=[SMEM] * 2
            + [by_step((per, width)), by_step((STEP_SLOTS, rows, width)), by_step((STEP_SLOTS, rows, width))]
            + [whole((micros, rows, width))] * 2
            + [by_step((per, width))] * 2
            + [ANY, whole((1, width))]
            + table_specs,
            out_specs=[by_step((per, 3 * width)), by_step((per, width)), whole((8, width))],
            out_shape=[sds((total, 3 * width), BF16), sds((total, width), BF16), sds((8, width), F32)],
            scratch_shapes=[
                pltpu.VMEM((width, 3 * width), BF16),
                pltpu.VMEM((per, width), F32),
                pltpu.SemaphoreType.DMA,
            ],
            compiler_params=params(),
            name="input",
        )(lengths, dealing, dq, dk, dv, ret_next, ret_prev, x, mid_grad, w_all, gain_pre, *tables)
        terms = jnp.stack([jnp.sum(pre_term, axis=0), jnp.sum(mid_term, axis=0)], axis=1)
        terms = jnp.pad(terms, ((0, 0), (0, PAIR - 2)))
        grads = [nn(normed_two_t, exp_grad), nn(ffn_grad_t, hid), nn(attended_t, attn_grad), nn(normed_one_t, delta), terms]
        grads = jnp.concatenate([g.astype(BF16) for g in grads], axis=1)
        block = lax.psum_scatter(grads, ("dp", "fsdp"), scatter_dimension=0, tiled=True).astype(F32)
        expand_sum, contract_sum, proj_sum, qkv_sum, gain_sum = [block[:, begin:end] for begin, end in cuts]
    return (
        result.reshape(inputs.shape),
        input_grad.reshape(inputs.shape),
        qkv_sum,
        proj_sum,
        expand_sum,
        contract_sum.T,
        gain_sum[:, 0],
        gain_sum[:, 1],
    )


def solution(mesh):
    both = ("dp", "fsdp")
    return jax.shard_map(
        local,
        mesh=mesh,
        in_specs=(
            P(None, both, None), P(None, both, None),
            P(both, None), P(both, None), P(both, None), P(None, both), P(both), P(both),
            P(None, "dp", None), P(None, both), P(None, None, both), P(None, both),
        ),
        out_specs=(
            P(None, both, None), P(None, both, None),
            P(both, None), P(both, None), P(both, None), P(None, both), P(both), P(both),
        ),
        check_vma=False,
    )
```
